128 devices in a mesh: fine: 32 (over z, x, core), coarse: 4 (over y).
Axes of the slice: x: 4, y: 4, z: 4, core: 2. Of those that a mesh axis runs over, the one named last changes fastest.
Arguments:
- loads: float32 [12, 256, 32, 256], P(None, 'fine', 'coarse'), may hold values from -6 to 6
- rotations: float32 [9, 256, 32, 256], P(None, 'fine', 'coarse'), may hold values from -1 to 1, as said below
- occupancy: int32 [256, 32, 256], P('fine', 'coarse'), may hold values 0 or 1
- element_matrix: float32 [24, 24], replicated, as said below
- line_inverse: bfloat16 [16, 128, 384, 384], P('coarse', 'fine')
Outputs:
- displacement: float32 [12, 256, 32, 256], P(None, 'fine', 'coarse')
- residual: float32 [12, 256, 32, 256], P(None, 'fine', 'coarse')
The draws below stay inside these ranges and needn't reach their ends.
Inputs may be any that keep to these rules, and one draw needn't show every extreme that they name: `rotations`: each element's nine entries form a rotation matrix. `element_matrix`: symmetric positive definite.
All inputs are finite; a program needn't handle non-finite values. No bound on the sum of `occupancy` on one device may be relied on, other than what follows from the above.
Results may differ from the reference program's by a relative error of at most 0.0041.
Values may be sent and summed in bfloat16 or wider, within the bound.
No kernel may reach another device: no remote copies, remote signals or barrier semaphores. Data moves between devices by JAX's collectives and lax.ppermute only.
A program may use at most 128 MiB of HBM per device.

```python
import jax
import jax.numpy as jnp
from jax import lax

EX = 8
EZ = 256
CASES = 4
NX = 256
NY = 32
LINE = 384


def draw_rotations(key, part):
    quats = jax.random.normal(key, (4, NX, NY, EZ), jnp.float32)
    quats = quats / jnp.sqrt(jnp.sum(quats * quats, axis=0, keepdims=True) + 1e-12)
    wpart, xpart, ypart, zpart = (quats[0], quats[1], quats[2], quats[3])
    rows = [1 - 2 * (ypart * ypart + zpart * zpart), 2 * (xpart * ypart - wpart * zpart), 2 * (xpart * zpart + wpart * ypart), 2 * (xpart * ypart + wpart * zpart), 1 - 2 * (xpart * xpart + zpart * zpart), 2 * (ypart * zpart - wpart * xpart), 2 * (xpart * zpart - wpart * ypart), 2 * (ypart * zpart + wpart * xpart), 1 - 2 * (xpart * xpart + ypart * ypart)]
    return jnp.clip(jnp.stack(rows), -1.0, 1.0).astype(jnp.float32)


def draw_element_matrix(key, part):
    factor = jax.random.normal(key, (24, 24), jnp.float32)
    return (jnp.dot(factor, factor.T) / 2.0 + 2.5 * jnp.eye(24, dtype=jnp.float32)).astype(jnp.float32)


def draw_line_inverse(key, part):
    noise = jax.random.normal(key, (NY // 2, EZ // 2, LINE, LINE), jnp.float32) * (0.4 / LINE ** 0.5)
    blocks = noise + 0.4 * jnp.eye(LINE, dtype=jnp.float32)
    return blocks.astype(jnp.bfloat16)


def place_ends(values, own_key, least, top_value):
    longest = values.shape.index(max(values.shape))
    spots = []
    for shift in (0, 1):
        where = [jax.random.randint(jax.random.fold_in(own_key, axis), (), 0, length) for axis, length in enumerate(values.shape)]
        where[longest] = (where[longest] + shift) % values.shape[longest]
        spots.append(tuple(where))
    return values.at[spots[0]].set(least).at[spots[1]].set(top_value)


def block_scale(stream_key, dims, cuts, low, top_value):
    def one(dim, parts):
        steps = jax.random.uniform(jax.random.fold_in(jax.random.fold_in(stream_key, 6), dim), (parts,), jnp.float32, low / len(cuts), top_value / len(cuts))
        return jnp.repeat(jnp.exp(steps), dims[dim] // parts).reshape((-1,) + (1,) * (len(dims) - dim - 1))

    factor_of = one(*cuts[0])
    for cut in cuts[1:]:
        factor_of = factor_of * one(*cut)
    return factor_of


def normal_values(own_key, extent, width, limit, cuts=(), kind=jnp.bfloat16):
    result = width * jax.random.normal(own_key, extent, jnp.float32)
    if cuts:
        result = result * block_scale(own_key, extent, cuts, -0.22, 0.18)
    return jnp.clip(result, -limit, limit).astype(kind)


def setup_inputs(seed: int = 0) -> dict:
    seeds = jax.random.split(jax.random.key(seed), 6)
    return {
        "loads": normal_values(seeds[0], (3 * CASES, NX, NY, EZ), 1.0, 6.0, ((1, 32), (2, 4)), jnp.float32),
        "rotations": draw_rotations(jax.random.fold_in(seeds[5], 71), 0),
        "occupancy": place_ends((jax.random.randint(seeds[2], (NX, NY, EZ), 0, 10) < 1).astype(jnp.int32), jax.random.fold_in(seeds[2], 1), 0, 1),
        "element_matrix": draw_element_matrix(jax.random.fold_in(seeds[5], 71), 0),
        "line_inverse": draw_line_inverse(jax.random.fold_in(seeds[5], 71), 0),
    }


relax_step = 0.1
spring = 0.1
highest = lax.Precision.HIGHEST


def apply_rotation(rotate, values, transpose):
    outputs = []
    for out_index in range(3):
        total = None
        for in_index in range(3):
            if transpose:
                entry = rotate[in_index, out_index]
            else:
                entry = rotate[out_index, in_index]
            term = entry[None, None] * values[:, in_index]
            total = term if total is None else total + term
        outputs.append(total)
    return jnp.stack(outputs, 1)


def element_apply(nodes, element_data, stiffness):
    span_x = nodes.shape[1] - 2
    span_y = nodes.shape[2] - 2
    depth = nodes.shape[3]
    closed = jnp.pad(nodes, ((0, 0), (0, 0), (0, 0), (0, 1)))
    displace = closed.reshape(3, 4, span_x + 2, span_y + 2, depth + 1)
    rotate = element_data[:9].reshape(3, 3, span_x + 1, span_y + 1, depth)
    weight = element_data[9]
    pieces = []
    for corner in range(8):
        off_x, off_y, off_z = corner % 2, (corner // 2) % 2, corner // 4
        pieces.append(displace[:, :, off_x:off_x + span_x + 1, off_y:off_y + span_y + 1, off_z:off_z + depth])
    gathered = jnp.stack(pieces)
    local = apply_rotation(rotate, gathered, True)
    forces = jnp.dot(stiffness, local.reshape(24, -1), precision=highest, preferred_element_type=jnp.float32).reshape(local.shape)
    turned = apply_rotation(rotate, forces, False) * weight
    total = spring * displace[:, :, 1:span_x + 1, 1:span_y + 1, :depth]
    for corner in range(8):
        off_x, off_y, off_z = corner % 2, (corner // 2) % 2, corner // 4
        part = turned[corner][:, :, 1 - off_x:1 - off_x + span_x, 1 - off_y:1 - off_y + span_y, :]
        if off_z:
            part = jnp.pad(part[..., :-1], ((0, 0), (0, 0), (0, 0), (0, 0), (1, 0)))
        total = total + part
    return total


def prolong(coarse_field):
    three, cases, size_x, size_y, size_z = coarse_field.shape
    grown = jnp.broadcast_to(coarse_field[:, :, :, None, :, None, :, None], (three, cases, size_x, 2, size_y, 2, size_z, 2))
    return grown.reshape(three, cases, 2 * size_x, 2 * size_y, 2 * size_z)


def reference(loads, rotations, occupancy, element_matrix, line_inverse):
    weight = 0.02 + 0.98 * occupancy.astype(jnp.float32)
    element_data = jnp.concatenate([rotations, weight[None]], 0)
    element_pad = jnp.pad(element_data, ((0, 0), (1, 0), (1, 0), (0, 0)))
    node_pad = jnp.pad(loads, ((0, 0), (1, 1), (1, 1), (0, 0)))
    blocks = NX // EX

    def one_block(index):
        nodes = lax.dynamic_slice_in_dim(node_pad, index * EX, EX + 2, 1)
        elems = lax.dynamic_slice_in_dim(element_pad, index * EX, EX + 1, 1)
        return element_apply(nodes, elems, element_matrix)

    image = lax.map(one_block, jnp.arange(blocks, dtype=jnp.int32))
    image = jnp.moveaxis(image, 0, 2).reshape(3, 4, NX, NY, EZ)
    given = loads.reshape(3, 4, NX, NY, EZ)
    residual = given - relax_step * image
    coarse = residual.reshape(3, 4, NX // 2, 2, NY // 2, 2, EZ // 2, 2).sum(axis=(3, 5, 7))
    coarse = coarse.astype(jnp.bfloat16)
    lines = jnp.transpose(coarse, (1, 3, 4, 0, 2)).reshape(4, NY // 2, EZ // 2, LINE)

    def solve_row(pair):
        inverse_row, vectors = pair
        return jnp.einsum("zmn,czn->czm", inverse_row.astype(jnp.float32), vectors.astype(jnp.float32), precision=highest)

    solved = lax.map(solve_row, (line_inverse, jnp.moveaxis(lines, 1, 0)))
    correction = jnp.moveaxis(solved, 0, 1).astype(jnp.bfloat16)
    correction = correction.reshape(4, NY // 2, EZ // 2, 3, NX // 2)
    correction = jnp.transpose(correction, (3, 0, 4, 1, 2)).astype(jnp.float32)
    displacement = relax_step * given + prolong(correction)
    return displacement.reshape(12, NX, NY, EZ), residual.reshape(12, NX, NY, EZ)
```

```python
import functools

import jax
import jax.numpy as jnp
import ml_dtypes
import numpy as np
from jax import lax
from jax.experimental import pallas as pl
from jax.experimental.pallas import tpu as pltpu
from jax.sharding import PartitionSpec as P

relax_step = 0.1
spring = 0.1
bf16 = jnp.bfloat16
f32 = jnp.float32
FINE = 32
COARSE = 4


def swaps(count, first):
    target = list(range(count))
    for i in range(first, count - 1, 2):
        target[i], target[i + 1] = i + 1, i
    return [(i, target[i]) for i in range(count)]


def tables():
    n = np.arange(384)
    n_i, n_f, n_x = n // 128, n % 128 // 4, n % 4
    r = np.arange(128)
    r_x, r_y = r % 16 // 8 * 2 + r % 2, r % 8 // 2
    slots = np.arange(32)
    rows = np.arange(256)
    z = np.arange(256)
    spread = n_f[:, None] == slots[None]
    keep, fold, lift = [], [], []
    for half in range(2):
        r_q = r // 16 + 6 * half
        keep.append((r[None] < 96) & (n_i[:, None] == r_q[None] // 4) & (n_x[:, None] == r_x[None]))
        for zz in range(4):
            to = r_y * 16 + zz * 4 + r_q % 4
            fold.append((r[:, None] < 96) & (to[:, None] == r[None]))
        mine = rows[:, None] % 8 // 4 == half
        lift.append(mine & (rows[:, None] // 8 * 4 + rows[:, None] % 4 == z[None] // 2))
    d_q, d_x, d_y = n // 32, n % 32 // 8, n % 8 // 2
    grown = (d_q[:, None] % 6 == r[None] // 16) & (d_x[:, None] == r_x[None]) & (d_y[:, None] == r_y[None])
    as_bf16 = lambda a: np.asarray(a, np.float32).astype(ml_dtypes.bfloat16)
    return {
        "spread": as_bf16(spread),
        "gather": as_bf16(spread.T),
        "keep": as_bf16(np.stack(keep)),
        "fold": as_bf16(np.stack(fold)),
        "lift": as_bf16(np.stack(lift)),
        "grown": as_bf16(grown),
    }


def rooted(occupancy):
    return jnp.sqrt(0.02 + 0.98 * occupancy.astype(f32))


def row_index():
    return lax.broadcasted_iota(jnp.int32, (8, 256), 0)


def next_z(v):
    lane = lax.broadcasted_iota(jnp.int32, v.shape, 1)
    return jnp.where(lane == 255, 0.0, pltpu.roll(v, 255, 1))


def past_z(v):
    lane = lax.broadcasted_iota(jnp.int32, v.shape, 1)
    return jnp.where(lane == 0, 0.0, pltpu.roll(v, 1, 1))


def x_faces_kernel(
    loads_ref, rot_ref, occ_ref, matrix_ref, one_ref, two_ref, loads_out, rot_out, occ_out, matrix_out, arrived
):
    face = [
        pltpu.make_async_copy(loads_ref.at[:, 0], loads_out.at[:, 0], arrived.at[0]),
        pltpu.make_async_copy(loads_ref.at[:, 7], loads_out.at[:, 7], arrived.at[1]),
        pltpu.make_async_copy(rot_ref.at[:, 7], rot_out.at[:, 7], arrived.at[2]),
        pltpu.make_async_copy(occ_ref, occ_out, arrived.at[3]),
    ]
    rest = [
        pltpu.make_async_copy(loads_ref.at[:, 1:7], loads_out.at[:, 1:7], arrived.at[4]),
        pltpu.make_async_copy(rot_ref.at[:, 0:7], rot_out.at[:, 0:7], arrived.at[5]),
        pltpu.make_async_copy(matrix_ref, matrix_out, arrived.at[6]),
    ]
    for copy in face + rest:
        copy.start()
    even = lax.axis_index("fine") % 2 == 0
    for copy in face:
        copy.wait()
    weight = rooted(occ_out[7])
    for q in range(12):
        low, high = loads_out[q, 0], loads_out[q, 7]
        one_ref[q] = jnp.where(even, high, low).astype(bf16)
        two_ref[q] = jnp.where(even, low, high).astype(bf16)
    for k in range(9):
        scaled = (rot_out[k, 7] * weight).astype(bf16)
        one_ref[12 + k] = scaled
        two_ref[12 + k] = scaled
    for copy in rest:
        copy.wait()


def x_sides(one_ref, two_ref, k):
    place = lax.axis_index("fine")
    even = place % 2 == 0
    one, two = one_ref[k].astype(f32), two_ref[k].astype(f32)
    low = jnp.where(place == 0, 0.0, jnp.where(even, two, one))
    high = jnp.where(place == FINE - 1, 0.0, jnp.where(even, one, two))
    return low, high


def rows_kernel(loads_ref, rot_ref, occ_ref, matrix_ref, first_ref, last_ref, stiff_ref):
    zero = jnp.zeros((1, 256), f32)
    zeros = jnp.zeros((7, 256), f32)
    occ = [rooted(occ_ref[x]) for x in range(8)]
    for q in range(12):
        planes = [loads_ref[q, x] for x in range(8)]
        first_ref[q] = jnp.concatenate([zero] + [p[0:1] for p in planes] + [zeros], 0)
        last_ref[q] = jnp.concatenate([zero] + [p[7:8] for p in planes] + [zeros], 0)
    for k in range(9):
        planes = [rot_ref[k, x] * occ[x] for x in range(8)]
        last_ref[12 + k] = jnp.concatenate([zero] + [p[7:8] for p in planes] + [zeros], 0)
    tall = lax.broadcasted_iota(jnp.int32, (192, 24), 0) // 8
    copy = (tall == lax.broadcasted_iota(jnp.int32, (192, 24), 1)).astype(bf16)
    same = lax.broadcasted_iota(jnp.int32, (192, 192), 0) % 8
    same = same == lax.broadcasted_iota(jnp.int32, (192, 192), 1) % 8
    whole_matrix = matrix_ref[...]
    main = whole_matrix.astype(bf16)
    rest = (whole_matrix - main.astype(f32)).astype(bf16)
    for slot, part in ((0, main), (1, rest)):
        wide = jnp.dot(copy, part, preferred_element_type=f32).astype(bf16)
        wide = lax.dot_general(wide, copy, (((1,), (1,)), ((), ())), preferred_element_type=f32)
        stiff_ref[slot] = jnp.where(same, wide, 0.0).astype(bf16)


def y_faces_kernel(first_ref, last_ref, px1_ref, px2_ref, one_ref, two_ref, near_ref, far_ref):
    even = lax.axis_index("coarse") % 2 == 0
    row = lax.broadcasted_iota(jnp.int32, (16, 256), 0)

    def ends(own, low, high):
        return jnp.where(row == 0, low, jnp.where(row == 9, high, own))

    for q in range(12):
        low, high = x_sides(px1_ref, px2_ref, q)
        first = ends(first_ref[q], low[0:1], high[0:1])
        last = ends(last_ref[q], low[7:8], high[7:8])
        near_ref[q] = first
        one_ref[q] = jnp.where(even, last, first).astype(bf16)
        two_ref[q] = jnp.where(even, first, last).astype(bf16)
    for k in range(9):
        low, _ = x_sides(px1_ref, px2_ref, 12 + k)
        last = jnp.where(row == 0, low[7:8], last_ref[12 + k])
        far_ref[k] = last
        one_ref[12 + k] = last.astype(bf16)
        two_ref[12 + k] = last.astype(bf16)


def turn_in(scale, nodes):
    return [
        scale[i] * nodes[0] + scale[3 + i] * nodes[1] + scale[6 + i] * nodes[2] for i in range(3)
    ]


def turn_out(scale, forces):
    return [
        scale[3 * i] * forces[0] + scale[3 * i + 1] * forces[1] + scale[3 * i + 2] * forces[2]
        for i in range(3)
    ]


def element_forces(stiff_ref, local, scale, pick):
    held, at = [], 0
    for corner in range(8):
        got = pick(corner)
        held += [jnp.zeros((8, 256), f32)] * 3 if got is None else turn_in(scale, got)
        while len(held) >= 2:
            pair = jnp.concatenate(held[:2], 0)
            main = pair.astype(bf16)
            local[0, 16 * at : 16 * at + 16] = main
            local[1, 16 * at : 16 * at + 16] = (pair - main.astype(f32)).astype(bf16)
            held, at = held[2:], at + 1
    main, rest = stiff_ref[0], stiff_ref[1]
    out = jnp.dot(main, local[0], preferred_element_type=f32)
    out = out + jnp.dot(rest, local[0], preferred_element_type=f32)
    return out + jnp.dot(main, local[1], preferred_element_type=f32)


def corner_rows(out, corner):
    return [out[8 * (3 * corner + j) : 8 * (3 * corner + j) + 8] for j in range(3)]


def put_nodes(nodes, p, q, v):
    up = jnp.where(row_index() == 7, 0.0, pltpu.roll(v, 7, 0))
    nodes[p, 0, q] = v
    nodes[p, 1, q] = up
    nodes[p, 2, q] = next_z(v)
    nodes[p, 3, q] = next_z(up)


def settle(sides):
    own = sides[0] + past_z(sides[2])
    upper = sides[1] + past_z(sides[3])
    return own + jnp.where(row_index() == 0, 0.0, pltpu.roll(upper, 1, 0))


def picker(nodes, p, case):
    def pick(corner):
        off_x, off_y, off_z = corner % 2, corner // 2 % 2, corner // 4
        return [nodes[p + off_x, off_y + 2 * off_z, j * 4 + case] for j in range(3)]

    return pick


def inner_kernel(start, count, loads_ref, rot_ref, occ_ref, stiff_ref, force_ref, nodes, carry, local):
    @pl.loop(0, count + 1)
    def _(p):
        for q in range(12):
            put_nodes(nodes, p, q, loads_ref[q, start + p])

    carry[...] = jnp.zeros_like(carry)

    @pl.loop(0, count)
    def _(e):
        weight = rooted(occ_ref[start + e])
        scale = [rot_ref[k, start + e] * weight for k in range(9)]
        for case in range(4):
            out = element_forces(stiff_ref, local.at[case], scale, picker(nodes, e, case))
            total = [[None] * 4 for _ in range(3)]
            for corner in range(8):
                turned = turn_out(scale, corner_rows(out, corner))
                for i in range(3):
                    q = i * 4 + case
                    if corner % 2 == 0:
                        total[i][corner // 2] = turned[i] + carry[corner // 2, q]
                    else:
                        carry[corner // 2, q] = turned[i]
            for i in range(3):
                force_ref[i * 4 + case, e] = settle(total[i])

    for q in range(12):
        force_ref[q, count] = settle([carry[side, q] for side in range(4)])


def x_edges_kernel(
    low_ref, high_ref, rot_ref, occ_ref, px1_ref, px2_ref, stiff_ref, force_ref, nodes, scales, local
):
    weight = rooted(occ_ref[0])
    for q in range(12):
        low, high = x_sides(px1_ref, px2_ref, q)
        for p, v in enumerate((low, low_ref[q, 0], high_ref[q, 0], high)):
            put_nodes(nodes, p, q, v)
    for k in range(9):
        low, _ = x_sides(px1_ref, px2_ref, 12 + k)
        scales[0, k] = low
        scales[1, k] = rot_ref[k, 0] * weight
    for edge in range(2):
        scale = [scales[edge, k] for k in range(9)]
        for case in range(4):
            at = 4 * edge + case
            out = element_forces(stiff_ref, local.at[at], scale, picker(nodes, 2 * edge, case))
            sides = [turn_out(scale, corner_rows(out, 2 * side + 1 - edge)) for side in range(4)]
            for i in range(3):
                force_ref[edge, i * 4 + case] = settle([side[i] for side in sides])


def finish_kernel(
    loads_ref,
    py1_ref,
    py2_ref,
    near_ref,
    far_ref,
    stiff_ref,
    lift_ref,
    inner1_ref,
    inner2_ref,
    edges_ref,
    residual_ref,
    coarse_ref,
    below,
    above,
    low0,
    low1,
    high0,
    high1,
    ends,
    made,
    local,
    sums,
    sent,
):
    row = row_index()
    place = lax.axis_index("coarse")
    even = place % 2 == 0
    for k in range(21):
        one, two = py1_ref[k].astype(f32), py2_ref[k].astype(f32)
        below[k] = jnp.where(place == 0, 0.0, jnp.where(even, two, one))
        if k < 12:
            above[k] = jnp.where(place == COARSE - 1, 0.0, jnp.where(even, one, two))

    for upper in range(2):
        scale = [far_ref[k, 0:8] if upper else below[12 + k, 0:8] for k in range(9)]
        for case in range(4):

            def pick(corner):
                off_x, off_y, off_z = corner % 2, corner // 2 % 2, corner // 4
                if upper and not off_y:
                    return None
                source = above if upper else near_ref if off_y else below
                got = [source[j * 4 + case, off_x : off_x + 8] for j in range(3)]
                return [next_z(v) for v in got] if off_z else got

            out = element_forces(stiff_ref, local.at[4 * upper + case], scale, pick)
            for off_x, target in ((0, (low0, high0)[upper]), (1, (low1, high1)[upper])):
                flat = turn_out(scale, corner_rows(out, off_x + 2 - 2 * upper))
                tall = turn_out(scale, corner_rows(out, off_x + 6 - 2 * upper))
                for i in range(3):
                    target[i * 4 + case] = flat[i] + past_z(tall[i])

    lower = row < 4
    scale = [jnp.where(lower, below[12 + k, 8:9], far_ref[k, 8:9]) for k in range(9)]

    def pick_last(corner):
        off_x, off_y, off_z = corner % 2, corner // 2 % 2, corner // 4
        at = 8 + off_x
        got = []
        for j in range(3):
            source = near_ref if off_y else below
            rows = [source[j * 4 + case, at : at + 1] for case in range(4)]
            if off_y:
                rows += [above[j * 4 + case, at : at + 1] for case in range(4)]
            else:
                rows += [jnp.zeros((4, 256), f32)]
            got.append(jnp.concatenate(rows, 0))
        return [next_z(v) for v in got] if off_z else got

    out = element_forces(stiff_ref, local.at[8], scale, pick_last)
    flat = [jnp.where(lower, u, v) for u, v in zip(corner_rows(out, 2), corner_rows(out, 0))]
    tall = [jnp.where(lower, u, v) for u, v in zip(corner_rows(out, 6), corner_rows(out, 4))]
    flat, tall = turn_out(scale, flat), turn_out(scale, tall)
    for i in range(3):
        ends[i] = flat[i] + past_z(tall[i])

    def residual_of(q, x, force):
        if x < 7:
            first, last = low0[q, x + 1 : x + 2], high0[q, x + 1 : x + 2]
        else:
            case = q % 4
            first, last = ends[q // 4, case : case + 1], ends[q // 4, 4 + case : 5 + case]
        first = first + low1[q, x : x + 1]
        last = last + high1[q, x : x + 1]
        force = force + jnp.where(row == 0, first, 0.0) + jnp.where(row == 7, last, 0.0)
        given = loads_ref[q, x]
        left = given - relax_step * (spring * given + force)
        made[q, x] = left
        return left

    split = inner1_ref.shape[1] - 1
    copies = [pltpu.make_async_copy(made.at[q], residual_ref.at[q], sent.at[q]) for q in range(12)]
    for q in range(12):
        planes = []
        for x in range(8):
            force = inner1_ref[q, x] if x <= split else inner2_ref[q, x - split]
            if x == split:
                force = force + inner2_ref[q, 0]
            if x in (0, 7):
                force = force + edges_ref[x // 7, q]
            planes.append(residual_of(q, x, force))
        copies[q].start()
        for half in range(2):
            s0 = planes[4 * half] + planes[4 * half + 1]
            s1 = planes[4 * half + 2] + planes[4 * half + 3]
            t0 = s0 + pltpu.roll(s0, 7, 0)
            t1 = s1 + pltpu.roll(s1, 1, 0)
            at = 16 * (q % 6) + 8 * half
            sums[q // 6, at : at + 8] = jnp.where(row % 2 == 0, t0, t1)
    nt = (((1,), (1,)), ((), ()))
    coarse = None
    for half in range(2):
        sums[half, 96:128] = jnp.zeros((32, 256), f32)
        every = sums[half]
        main = every.astype(bf16)
        rest = (every - main.astype(f32)).astype(bf16)
        for part in (main, rest):
            term = lax.dot_general(lift_ref[half], part, nt, preferred_element_type=f32)
            coarse = term if coarse is None else coarse + term
    coarse_ref[...] = coarse.astype(bf16)
    for copy in copies:
        copy.wait()


def lines_kernel(
    got_ref, inverse_ref, spread_ref, gather_ref, keep_ref, fold_ref, sent_ref, rows, back
):
    nt = (((1,), (1,)), ((), ()))
    rows[...] = got_ref[...].astype(f32)
    vectors = jnp.zeros((384, 128), f32)
    for half in range(2):
        keep = keep_ref[half].astype(f32)
        for zz in range(4):
            part = rows[pl.ds(4 * half + zz, 32, stride=8), :].astype(bf16)
            wide = jnp.dot(spread_ref[...], part, preferred_element_type=f32) * keep
            fold = fold_ref[4 * half + zz]
            vectors = vectors + jnp.dot(wide.astype(bf16), fold, preferred_element_type=f32)
    vectors = vectors.astype(bf16)
    line = lax.broadcasted_iota(jnp.int32, (384, 128), 1) // 4
    solved = jnp.zeros((384, 128), f32)
    for k in range(16):
        one = jnp.dot(inverse_ref[k], vectors, preferred_element_type=f32)
        solved = jnp.where(line == k, one, solved)
    solved = solved.astype(bf16)
    for half in range(2):
        keep = keep_ref[half].astype(f32)
        for zz in range(4):
            fold = fold_ref[4 * half + zz]
            wide = lax.dot_general(solved, fold, nt, preferred_element_type=f32) * keep
            back[pl.ds(4 * half + zz, 32, stride=8), :] = jnp.dot(
                gather_ref[...], wide.astype(bf16), preferred_element_type=f32
            )
    sent_ref[...] = back[...].astype(bf16)


def correct_kernel(loads_ref, back_ref, grown_ref, lift_ref, out_ref, made, sent):
    nt = (((1,), (1,)), ((), ()))
    copies = [pltpu.make_async_copy(made.at[q], out_ref.at[q], sent.at[q]) for q in range(12)]
    tall = lax.dot_general(grown_ref[...], back_ref[...], nt, preferred_element_type=f32).astype(bf16)
    for half in range(2):
        mine = tall[192 * half : 192 * half + 192]
        coarse = jnp.dot(mine, lift_ref[half], preferred_element_type=f32)
        for q in range(6 * half, 6 * half + 6):
            for part in range(4):
                at = 32 * (q % 6) + 8 * part
                added = coarse[at : at + 8]
                for x in (2 * part, 2 * part + 1):
                    made[q, x] = relax_step * loads_ref[q, x] + added
            copies[q].start()
    for copy in copies:
        copy.wait()


def whole(count):
    return [pl.BlockSpec(memory_space=pltpu.VMEM)] * count


def params(mib):
    return pltpu.CompilerParams(vmem_limit_bytes=mib << 20)


def cost(us):
    return pl.CostEstimate(flops=0, bytes_accessed=int(us * 3.0e6), transcendentals=0)


def body(loads, rotations, occupancy, element_matrix, line_inverse):
    table = {name: jnp.asarray(value) for name, value in tables().items()}
    shape = jax.ShapeDtypeStruct
    face = shape((21, 8, 256), bf16)
    plane = lambda count, at: pl.BlockSpec((count, 1, 8, 256), lambda i: (0, at, 0, 0))
    px1, px2, loads, rotations, occupancy, matrix = pl.pallas_call(
        x_faces_kernel,
        in_specs=[pl.BlockSpec(memory_space=pltpu.MemorySpace.HBM)] * 4,
        out_specs=whole(6),
        out_shape=(
            face,
            face,
            shape(loads.shape, f32),
            shape(rotations.shape, f32),
            shape(occupancy.shape, jnp.int32),
            shape((24, 24), f32),
        ),
        scratch_shapes=[pltpu.SemaphoreType.DMA((7,))],
        compiler_params=pltpu.CompilerParams(vmem_limit_bytes=FIRST),
        name="x_faces",
    )(*(pltpu.with_memory_space_constraint(a, pltpu.MemorySpace.HBM) for a in (loads, rotations, occupancy, element_matrix)))
    px1 = lax.ppermute(px1, "fine", swaps(FINE, 0))
    px2 = lax.ppermute(px2, "fine", swaps(FINE, 1))
    first, last, stiff = pl.pallas_call(
        rows_kernel,
        in_specs=whole(4),
        out_specs=whole(3),
        out_shape=(shape((12, 16, 256), f32), shape((21, 16, 256), f32), shape((2, 192, 192), bf16)),
        compiler_params=params(8),
        cost_estimate=cost(2),
        name="rows",
    )(loads, rotations, occupancy, matrix)

    def inner(start, count):
        return pl.pallas_call(
            functools.partial(inner_kernel, start, count),
            in_specs=whole(4),
            out_specs=whole(1)[0],
            out_shape=shape((12, count + 1, 8, 256), f32),
            scratch_shapes=[
                pltpu.VMEM((count + 1, 4, 12, 8, 256), f32),
                pltpu.VMEM((4, 12, 8, 256), f32),
                pltpu.VMEM((4, 2, 192, 256), bf16),
            ],
            compiler_params=params(12),
            cost_estimate=cost(0.8 * count),
            name=f"inner_{start}",
        )(loads, rotations, occupancy, stiff)

    inner1 = inner(0, SPLIT)
    first, inner1 = lax.optimization_barrier((first, inner1))
    face = shape((21, 16, 256), bf16)
    py1, py2, near, far = pl.pallas_call(
        y_faces_kernel,
        in_specs=whole(4),
        out_specs=whole(4),
        out_shape=(face, face, shape((12, 16, 256), f32), shape((9, 16, 256), f32)),
        compiler_params=params(8),
        name="y_faces",
    )(first, last, px1, px2)
    py1 = lax.ppermute(py1, "coarse", swaps(COARSE, 0))
    py2 = lax.ppermute(py2, "coarse", swaps(COARSE, 1))
    inner2 = inner(SPLIT, 7 - SPLIT)
    edges = pl.pallas_call(
        x_edges_kernel,
        grid=(1,),
        in_specs=[
            plane(12, 0),
            plane(12, 7),
            plane(9, 7),
            pl.BlockSpec((1, 8, 256), lambda i: (7, 0, 0)),
            pl.BlockSpec((21, 8, 256), lambda i: (0, 0, 0)),
            pl.BlockSpec((21, 8, 256), lambda i: (0, 0, 0)),
            pl.BlockSpec((2, 192, 192), lambda i: (0, 0, 0)),
        ],
        out_specs=pl.BlockSpec((2, 12, 8, 256), lambda i: (0, 0, 0, 0)),
        out_shape=shape((2, 12, 8, 256), f32),
        scratch_shapes=[
            pltpu.VMEM((4, 4, 12, 8, 256), f32),
            pltpu.VMEM((2, 9, 8, 256), f32),
            pltpu.VMEM((8, 2, 192, 256), bf16),
        ],
        compiler_params=params(12),
        cost_estimate=cost(1.6),
        name="x_edges",
    )(loads, loads, rotations, occupancy, px1, px2, stiff)
    tall = lambda count, rows: pltpu.VMEM((count, rows, 256), f32)
    residual, coarse = pl.pallas_call(
        finish_kernel,
        in_specs=whole(10),
        out_specs=[pl.BlockSpec(memory_space=pltpu.MemorySpace.HBM)] + whole(1),
        out_shape=(shape((12, 8, 8, 256), f32), shape((256, 128), bf16)),
        scratch_shapes=[
            tall(21, 16), tall(12, 16),
            tall(12, 8), tall(12, 8), tall(12, 8), tall(12, 8), tall(3, 8),
            pltpu.VMEM((12, 8, 8, 256), f32),
            pltpu.VMEM((9, 2, 192, 256), bf16),
            tall(2, 128),
            pltpu.SemaphoreType.DMA((12,)),
        ],
        compiler_params=params(16),
        name="finish",
    )(loads, py1, py2, near, far, stiff, table["lift"], inner1, inner2, edges)
    got = lax.all_to_all(coarse.reshape(32, 8, 128), "fine", 0, 0, tiled=True)
    sent = pl.pallas_call(
        lines_kernel,
        in_specs=whole(6),
        out_specs=whole(1)[0],
        out_shape=shape((256, 128), bf16),
        scratch_shapes=[
            pltpu.VMEM((256, 128), f32),
            pltpu.VMEM((256, 128), f32),
        ],
        compiler_params=params(16),
        name="lines",
    )(
        got.reshape(256, 128),
        line_inverse.reshape(16, 384, 384),
        *(table[k] for k in ("spread", "gather", "keep", "fold")),
    )
    back = lax.all_to_all(sent.reshape(32, 8, 128), "fine", 0, 0, tiled=True)
    displacement = pl.pallas_call(
        correct_kernel,
        in_specs=whole(4),
        out_specs=pl.BlockSpec(memory_space=pltpu.MemorySpace.HBM),
        out_shape=shape((12, 8, 8, 256), f32),
        scratch_shapes=[pltpu.VMEM((12, 8, 8, 256), f32), pltpu.SemaphoreType.DMA((12,))],
        compiler_params=params(12),
        name="correct",
    )(loads, back.reshape(256, 128), table["grown"], table["lift"])
    return displacement, residual


SPLIT = 3
FIRST = 8 << 20

def solution(mesh):
    in_specs = (
        P(None, "fine", "coarse", None),
        P(None, "fine", "coarse", None),
        P("fine", "coarse", None),
        P(),
        P("coarse", "fine", None, None),
    )
    out_specs = (P(None, "fine", "coarse", None), P(None, "fine", "coarse", None))
    return jax.shard_map(body, mesh=mesh, in_specs=in_specs, out_specs=out_specs, check_vma=False)
```

```python
import functools

import jax
import jax.numpy as jnp
import ml_dtypes
import numpy as np
from jax import lax
from jax.experimental import pallas as pl
from jax.experimental.pallas import tpu as pltpu
from jax.sharding import PartitionSpec as P

relax_step = 0.1
spring = 0.1
bf16 = jnp.bfloat16
f32 = jnp.float32
FINE = 32
COARSE = 4


def swaps(count, first):
    target = list(range(count))
    for i in range(first, count - 1, 2):
        target[i], target[i + 1] = i + 1, i
    return [(i, target[i]) for i in range(count)]


def tables():
    n = np.arange(384)
    n_i, n_f, n_x = n // 128, n % 128 // 4, n % 4
    r = np.arange(128)
    r_x, r_y = r % 16 // 8 * 2 + r % 2, r % 8 // 2
    slots = np.arange(32)
    rows = np.arange(256)
    z = np.arange(256)
    spread = n_f[:, None] == slots[None]
    keep, fold, lift = [], [], []
    for half in range(2):
        r_q = r // 16 + 6 * half
        keep.append((r[None] < 96) & (n_i[:, None] == r_q[None] // 4) & (n_x[:, None] == r_x[None]))
        for zz in range(4):
            to = r_y * 16 + zz * 4 + r_q % 4
            fold.append((r[:, None] < 96) & (to[:, None] == r[None]))
        mine = rows[:, None] % 8 // 4 == half
        lift.append(mine & (rows[:, None] // 8 * 4 + rows[:, None] % 4 == z[None] // 2))
    d_q, d_x, d_y = n // 32, n % 32 // 8, n % 8 // 2
    grown = (d_q[:, None] % 6 == r[None] // 16) & (d_x[:, None] == r_x[None]) & (d_y[:, None] == r_y[None])
    as_bf16 = lambda a: np.asarray(a, np.float32).astype(ml_dtypes.bfloat16)
    return {
        "spread": as_bf16(spread),
        "gather": as_bf16(spread.T),
        "keep": as_bf16(np.stack(keep)),
        "fold": as_bf16(np.stack(fold).reshape(4, 256, 128)),
        "lift": as_bf16(np.stack(lift)),
        "grown": as_bf16(grown),
    }


def rooted(occupancy):
    return jnp.sqrt(0.02 + 0.98 * occupancy.astype(f32))


def row_index():
    return lax.broadcasted_iota(jnp.int32, (8, 256), 0)


def next_z(v):
    lane = lax.broadcasted_iota(jnp.int32, v.shape, 1)
    return jnp.where(lane == 255, 0.0, pltpu.roll(v, 255, 1))


def past_z(v):
    lane = lax.broadcasted_iota(jnp.int32, v.shape, 1)
    return jnp.where(lane == 0, 0.0, pltpu.roll(v, 1, 1))


def x_faces_kernel(
    loads_ref, rot_ref, occ_ref, matrix_ref, one_ref, two_ref, loads_out, rot_out, occ_out, matrix_out, arrived
):
    face = [
        pltpu.make_async_copy(loads_ref.at[:, 0], loads_out.at[:, 0], arrived.at[0]),
        pltpu.make_async_copy(loads_ref.at[:, 7], loads_out.at[:, 7], arrived.at[1]),
        pltpu.make_async_copy(rot_ref.at[:, 7], rot_out.at[:, 7], arrived.at[2]),
        pltpu.make_async_copy(occ_ref, occ_out, arrived.at[3]),
    ]
    rest = [
        pltpu.make_async_copy(loads_ref.at[:, 1:7], loads_out.at[:, 1:7], arrived.at[4]),
        pltpu.make_async_copy(rot_ref.at[:, 0:7], rot_out.at[:, 0:7], arrived.at[5]),
        pltpu.make_async_copy(matrix_ref, matrix_out, arrived.at[6]),
    ]
    for copy in face + rest:
        copy.start()
    even = lax.axis_index("fine") % 2 == 0
    for copy in face:
        copy.wait()
    weight = rooted(occ_out[7])
    for q in range(12):
        low, high = loads_out[q, 0], loads_out[q, 7]
        one_ref[q] = jnp.where(even, high, low).astype(bf16)
        two_ref[q] = jnp.where(even, low, high).astype(bf16)
    for k in range(9):
        scaled = (rot_out[k, 7] * weight).astype(bf16)
        one_ref[12 + k] = scaled
        two_ref[12 + k] = scaled
    for copy in rest:
        copy.wait()


def x_sides(one_ref, two_ref, k):
    place = lax.axis_index("fine")
    even = place % 2 == 0
    one, two = one_ref[k].astype(f32), two_ref[k].astype(f32)
    low = jnp.where(place == 0, 0.0, jnp.where(even, two, one))
    high = jnp.where(place == FINE - 1, 0.0, jnp.where(even, one, two))
    return low, high


def rows_kernel(loads_ref, rot_ref, occ_ref, matrix_ref, first_ref, last_ref, stiff_ref):
    occ = [rooted(occ_ref[x]) for x in range(8)]
    for q in range(12):
        planes = [loads_ref[q, x] for x in range(8)]
        first_ref[q] = jnp.concatenate([p[0:1] for p in planes], 0)
        last_ref[q] = jnp.concatenate([p[7:8] for p in planes], 0)
    for k in range(9):
        planes = [rot_ref[k, x] * occ[x] for x in range(8)]
        last_ref[12 + k] = jnp.concatenate([p[7:8] for p in planes], 0)
    tall = lax.broadcasted_iota(jnp.int32, (192, 24), 0) // 8
    copy = (tall == lax.broadcasted_iota(jnp.int32, (192, 24), 1)).astype(bf16)
    same = lax.broadcasted_iota(jnp.int32, (192, 192), 0) % 8
    same = same == lax.broadcasted_iota(jnp.int32, (192, 192), 1) % 8
    whole_matrix = matrix_ref[...]
    main = whole_matrix.astype(bf16)
    rest = (whole_matrix - main.astype(f32)).astype(bf16)
    for slot, part in ((0, main), (1, rest)):
        wide = jnp.dot(copy, part, preferred_element_type=f32).astype(bf16)
        wide = lax.dot_general(wide, copy, (((1,), (1,)), ((), ())), preferred_element_type=f32)
        stiff_ref[slot] = jnp.where(same, wide, 0.0).astype(bf16)


def y_faces_kernel(first_ref, last_ref, px1_ref, px2_ref, one_ref, two_ref, near_ref, far_ref):
    even = lax.axis_index("coarse") % 2 == 0
    sides = [x_sides(px1_ref, px2_ref, k) for k in range(21)]

    def column(side, count, row, rows):
        picked = [sides[k][side][row : row + 1] for k in range(count)]
        return jnp.concatenate(picked + [jnp.zeros((rows - count, 256), f32)], 0)

    def send(tile, last, first):
        one_ref[tile] = jnp.where(even, last, first).astype(bf16)
        two_ref[tile] = jnp.where(even, first, last).astype(bf16)

    for k in range(21):
        last = last_ref[k]
        send(k, last, first_ref[k] if k < 12 else last)
    low_last = column(0, 21, 7, 24)
    near_low, high_last, near_high = column(0, 12, 0, 16), column(1, 12, 7, 16), column(1, 12, 0, 16)
    near_ref[0] = near_low
    near_ref[1] = near_high
    far_ref[...] = low_last[8:24]
    for tile in range(2):
        at = 8 * tile
        send(21 + tile, low_last[at : at + 8], near_low[at : at + 8])
        send(24 + tile, high_last[at : at + 8], near_high[at : at + 8])
    send(23, low_last[16:24], low_last[16:24])


def turn_in(scale, nodes):
    return [
        scale[i] * nodes[0] + scale[3 + i] * nodes[1] + scale[6 + i] * nodes[2] for i in range(3)
    ]


def turn_out(scale, forces):
    return [
        scale[3 * i] * forces[0] + scale[3 * i + 1] * forces[1] + scale[3 * i + 2] * forces[2]
        for i in range(3)
    ]


def element_forces(stiff_ref, local, scale, pick):
    held, at = [], 0
    for corner in range(8):
        got = pick(corner)
        held += [jnp.zeros((8, 256), f32)] * 3 if got is None else turn_in(scale, got)
        while len(held) >= 2:
            pair = jnp.concatenate(held[:2], 0)
            main = pair.astype(bf16)
            local[0, 16 * at : 16 * at + 16] = main
            local[1, 16 * at : 16 * at + 16] = (pair - main.astype(f32)).astype(bf16)
            held, at = held[2:], at + 1
    main, rest = stiff_ref[0], stiff_ref[1]
    out = jnp.dot(main, local[0], preferred_element_type=f32)
    out = out + jnp.dot(rest, local[0], preferred_element_type=f32)
    return out + jnp.dot(main, local[1], preferred_element_type=f32)


def corner_rows(out, corner):
    return [out[8 * (3 * corner + j) : 8 * (3 * corner + j) + 8] for j in range(3)]


def put_nodes(nodes, p, q, v):
    up = jnp.where(row_index() == 7, 0.0, pltpu.roll(v, 7, 0))
    nodes[p, 0, q] = v
    nodes[p, 1, q] = up
    nodes[p, 2, q] = next_z(v)
    nodes[p, 3, q] = next_z(up)


def settle(sides):
    own = sides[0] + past_z(sides[2])
    upper = sides[1] + past_z(sides[3])
    return own + jnp.where(row_index() == 0, 0.0, pltpu.roll(upper, 1, 0))


def picker(nodes, p, case):
    def pick(corner):
        off_x, off_y, off_z = corner % 2, corner // 2 % 2, corner // 4
        return [nodes[p + off_x, off_y + 2 * off_z, j * 4 + case] for j in range(3)]

    return pick


def inner_kernel(start, count, loads_ref, rot_ref, occ_ref, stiff_ref, force_ref, nodes, carry, local):
    @pl.loop(0, count + 1)
    def _(p):
        for q in range(12):
            put_nodes(nodes, p, q, loads_ref[q, start + p])

    carry[...] = jnp.zeros_like(carry)

    @pl.loop(0, count)
    def _(e):
        weight = rooted(occ_ref[start + e])
        scale = [rot_ref[k, start + e] * weight for k in range(9)]
        for case in range(4):
            out = element_forces(stiff_ref, local.at[case], scale, picker(nodes, e, case))
            total = [[None] * 4 for _ in range(3)]
            for corner in range(8):
                turned = turn_out(scale, corner_rows(out, corner))
                for i in range(3):
                    q = i * 4 + case
                    if corner % 2 == 0:
                        total[i][corner // 2] = turned[i] + carry[corner // 2, q]
                    else:
                        carry[corner // 2, q] = turned[i]
            for i in range(3):
                force_ref[i * 4 + case, e] = settle(total[i])

    for q in range(12):
        force_ref[q, count] = settle([carry[side, q] for side in range(4)])


def x_edges_kernel(
    low_ref, high_ref, rot_ref, occ_ref, px1_ref, px2_ref, stiff_ref, force_ref, nodes, scales, local
):
    weight = rooted(occ_ref[0])
    for q in range(12):
        low, high = x_sides(px1_ref, px2_ref, q)
        for p, v in enumerate((low, low_ref[q, 0], high_ref[q, 0], high)):
            put_nodes(nodes, p, q, v)
    for k in range(9):
        low, _ = x_sides(px1_ref, px2_ref, 12 + k)
        scales[0, k] = low
        scales[1, k] = rot_ref[k, 0] * weight
    for edge in range(2):
        scale = [scales[edge, k] for k in range(9)]
        for case in range(4):
            at = 4 * edge + case
            out = element_forces(stiff_ref, local.at[at], scale, picker(nodes, 2 * edge, case))
            sides = [turn_out(scale, corner_rows(out, 2 * side + 1 - edge)) for side in range(4)]
            for i in range(3):
                force_ref[edge, i * 4 + case] = settle([side[i] for side in sides])


def finish_kernel(
    loads_ref,
    first_ref,
    last_ref,
    py1_ref,
    py2_ref,
    near_ref,
    far_ref,
    stiff_ref,
    lift_ref,
    inner1_ref,
    inner2_ref,
    edges_ref,
    residual_ref,
    coarse_ref,
    below,
    above,
    low,
    high,
    made,
    local,
    sums,
    sent,
):
    row = row_index()
    place = lax.axis_index("coarse")
    even = place % 2 == 0
    for k in range(26):
        one, two = py1_ref[k].astype(f32), py2_ref[k].astype(f32)
        below[8 * k : 8 * k + 8] = jnp.where(place == 0, 0.0, jnp.where(even, two, one))
        above[8 * k : 8 * k + 8] = jnp.where(place == COARSE - 1, 0.0, jnp.where(even, one, two))

    def tile(source, k):
        return source[8 * k : 8 * k + 8]

    def single(source, at):
        return source[at : at + 1]

    lower = row < 4
    scale = [jnp.where(lower, single(below, 180 + k), single(far_ref, 4 + k)) for k in range(9)]

    def pick_first(corner):
        off_x, off_y, off_z = corner % 2, corner // 2 % 2, corner // 4
        got = []
        for j in range(3):
            rows = []
            for case in range(4):
                q = j * 4 + case
                if off_y:
                    rows.append(first_ref[q, 0:1] if off_x else near_ref[0, q : q + 1])
                else:
                    rows.append(single(below, 8 * q if off_x else 168 + q))
            if off_y:
                rows += [single(above, 8 * q if off_x else 168 + q) for q in range(4 * j, 4 * j + 4)]
            else:
                rows.append(jnp.zeros((4, 256), f32))
            got.append(jnp.concatenate(rows, 0))
        return [next_z(v) for v in got] if off_z else got

    out = element_forces(stiff_ref, local.at[8], scale, pick_first)
    flat = [jnp.where(lower, u, v) for u, v in zip(corner_rows(out, 3), corner_rows(out, 1))]
    tall = [jnp.where(lower, u, v) for u, v in zip(corner_rows(out, 7), corner_rows(out, 5))]
    flat, tall = turn_out(scale, flat), turn_out(scale, tall)
    ends = [flat[i] + past_z(tall[i]) for i in range(3)]

    for upper in range(2):
        scale = [last_ref[12 + k] if upper else tile(below, 12 + k) for k in range(9)]
        for case in range(4):

            def pick(corner):
                off_x, off_y, off_z = corner % 2, corner // 2 % 2, corner // 4
                if upper and not off_y:
                    return None
                got = []
                for q in (case, 4 + case, 8 + case):
                    if not upper and off_y:
                        v, past = first_ref[q], near_ref[1, q : q + 1]
                    else:
                        source = above if upper else below
                        v, past = tile(source, q), single(source, 192 + q)
                    got.append(jnp.where(row == 7, past, pltpu.roll(v, 7, 0)) if off_x else v)
                return [next_z(v) for v in got] if off_z else got

            out = element_forces(stiff_ref, local.at[4 * upper + case], scale, pick)
            sides = []
            for off_x in range(2):
                flat = turn_out(scale, corner_rows(out, off_x + 2 - 2 * upper))
                tall = turn_out(scale, corner_rows(out, off_x + 6 - 2 * upper))
                sides.append([flat[i] + past_z(tall[i]) for i in range(3)])
            at = 4 * upper + case
            for i in range(3):
                past = jnp.where(row == 0, ends[i][at : at + 1], pltpu.roll(sides[1][i], 1, 0))
                (low, high)[upper][i * 4 + case] = sides[0][i] + past

    def residual_of(q, x, force):
        force = force + jnp.where(row == 0, low[q, x : x + 1], 0.0)
        force = force + jnp.where(row == 7, high[q, x : x + 1], 0.0)
        given = loads_ref[q, x]
        left = given - relax_step * (spring * given + force)
        made[q, x] = left
        return left

    split = inner1_ref.shape[1] - 1
    copies = [pltpu.make_async_copy(made.at[q], residual_ref.at[q], sent.at[q]) for q in range(12)]
    for q in range(12):
        planes = []
        for x in range(8):
            force = inner1_ref[q, x] if x <= split else inner2_ref[q, x - split]
            if x == split:
                force = force + inner2_ref[q, 0]
            if x in (0, 7):
                force = force + edges_ref[x // 7, q]
            planes.append(residual_of(q, x, force))
        copies[q].start()
        for half in range(2):
            s0 = planes[4 * half] + planes[4 * half + 1]
            s1 = planes[4 * half + 2] + planes[4 * half + 3]
            t0 = s0 + pltpu.roll(s0, 7, 0)
            t1 = s1 + pltpu.roll(s1, 1, 0)
            at = 16 * (q % 6) + 8 * half
            sums[q // 6, at : at + 8] = jnp.where(row % 2 == 0, t0, t1)
    nt = (((1,), (1,)), ((), ()))
    coarse = None
    for half in range(2):
        sums[half, 96:128] = jnp.zeros((32, 256), f32)
        every = sums[half]
        main = every.astype(bf16)
        rest = (every - main.astype(f32)).astype(bf16)
        for part in (main, rest):
            term = lax.dot_general(lift_ref[half], part, nt, preferred_element_type=f32)
            coarse = term if coarse is None else coarse + term
    coarse_ref[...] = coarse.astype(bf16)
    for copy in copies:
        copy.wait()


def lines_kernel(
    got_ref, inverse_ref, spread_ref, gather_ref, keep_ref, fold_ref, sent_ref, rows, back
):
    nt = (((1,), (1,)), ((), ()))
    rows[...] = got_ref[...].astype(f32)
    vectors = jnp.zeros((384, 128), f32)
    for half in range(2):
        keep = keep_ref[half].astype(f32)
        keep = jnp.concatenate([keep, keep], 1)
        for pair in range(2 * half, 2 * half + 2):
            part = [rows[pl.ds(2 * pair + k, 32, stride=8), :] for k in range(2)]
            part = jnp.concatenate(part, 1).astype(bf16)
            wide = jnp.dot(spread_ref[...], part, preferred_element_type=f32) * keep
            vectors = vectors + jnp.dot(wide.astype(bf16), fold_ref[pair], preferred_element_type=f32)
    vectors = vectors.astype(bf16)
    line = lax.broadcasted_iota(jnp.int32, (384, 128), 1) // 4
    solved = jnp.zeros((384, 128), f32)
    for k in range(16):
        one = jnp.dot(inverse_ref[k], vectors, preferred_element_type=f32)
        solved = jnp.where(line == k, one, solved)
    solved = solved.astype(bf16)
    for half in range(2):
        keep = keep_ref[half].astype(f32)
        keep = jnp.concatenate([keep, keep], 1)
        for pair in range(2 * half, 2 * half + 2):
            wide = lax.dot_general(solved, fold_ref[pair], nt, preferred_element_type=f32) * keep
            part = jnp.dot(gather_ref[...], wide.astype(bf16), preferred_element_type=f32)
            for k in range(2):
                back[pl.ds(2 * pair + k, 32, stride=8), :] = part[:, 128 * k : 128 * k + 128]
    sent_ref[...] = back[...].astype(bf16)


def correct_kernel(loads_ref, back_ref, grown_ref, lift_ref, out_ref, made, sent):
    nt = (((1,), (1,)), ((), ()))
    copies = [pltpu.make_async_copy(made.at[q], out_ref.at[q], sent.at[q]) for q in range(12)]
    tall = lax.dot_general(grown_ref[...], back_ref[...], nt, preferred_element_type=f32).astype(bf16)
    for half in range(2):
        mine = tall[192 * half : 192 * half + 192]
        coarse = jnp.dot(mine, lift_ref[half], preferred_element_type=f32)
        for q in range(6 * half, 6 * half + 6):
            for part in range(4):
                at = 32 * (q % 6) + 8 * part
                added = coarse[at : at + 8]
                for x in (2 * part, 2 * part + 1):
                    made[q, x] = relax_step * loads_ref[q, x] + added
            copies[q].start()
    for copy in copies:
        copy.wait()


def whole(count):
    return [pl.BlockSpec(memory_space=pltpu.VMEM)] * count


def params(mib):
    return pltpu.CompilerParams(vmem_limit_bytes=mib << 20)


def cost(us):
    return pl.CostEstimate(flops=0, bytes_accessed=int(us * 3.0e6), transcendentals=0)


def body(loads, rotations, occupancy, element_matrix, line_inverse):
    table = {name: jnp.asarray(value) for name, value in tables().items()}
    shape = jax.ShapeDtypeStruct
    face = shape((21, 8, 256), bf16)
    plane = lambda count, at: pl.BlockSpec((count, 1, 8, 256), lambda i: (0, at, 0, 0))
    px1, px2, loads, rotations, occupancy, matrix = pl.pallas_call(
        x_faces_kernel,
        in_specs=[pl.BlockSpec(memory_space=pltpu.MemorySpace.HBM)] * 4,
        out_specs=whole(6),
        out_shape=(
            face,
            face,
            shape(loads.shape, f32),
            shape(rotations.shape, f32),
            shape(occupancy.shape, jnp.int32),
            shape((24, 24), f32),
        ),
        scratch_shapes=[pltpu.SemaphoreType.DMA((7,))],
        compiler_params=pltpu.CompilerParams(vmem_limit_bytes=FIRST),
        name="x_faces",
    )(*(pltpu.with_memory_space_constraint(a, pltpu.MemorySpace.HBM) for a in (loads, rotations, occupancy, element_matrix)))
    px1 = lax.ppermute(px1, "fine", swaps(FINE, 0))
    px2 = lax.ppermute(px2, "fine", swaps(FINE, 1))
    first, last, stiff = pl.pallas_call(
        rows_kernel,
        in_specs=whole(4),
        out_specs=whole(3),
        out_shape=(shape((12, 8, 256), f32), shape((21, 8, 256), f32), shape((2, 192, 192), bf16)),
        compiler_params=params(8),
        cost_estimate=cost(2),
        name="rows",
    )(loads, rotations, occupancy, matrix)

    def inner(start, count):
        return pl.pallas_call(
            functools.partial(inner_kernel, start, count),
            in_specs=whole(4),
            out_specs=whole(1)[0],
            out_shape=shape((12, count + 1, 8, 256), f32),
            scratch_shapes=[
                pltpu.VMEM((count + 1, 4, 12, 8, 256), f32),
                pltpu.VMEM((4, 12, 8, 256), f32),
                pltpu.VMEM((4, 2, 192, 256), bf16),
            ],
            compiler_params=params(12),
            cost_estimate=cost(0.8 * count),
            name=f"inner_{start}",
        )(loads, rotations, occupancy, stiff)

    inner1 = inner(0, SPLIT)
    first, inner1 = lax.optimization_barrier((first, inner1))
    face = shape((26, 8, 256), bf16)
    py1, py2, near, far = pl.pallas_call(
        y_faces_kernel,
        in_specs=whole(4),
        out_specs=whole(4),
        out_shape=(face, face, shape((2, 16, 256), f32), shape((16, 256), f32)),
        compiler_params=params(8),
        name="y_faces",
    )(first, last, px1, px2)
    py1 = lax.ppermute(py1, "coarse", swaps(COARSE, 0))
    py2 = lax.ppermute(py2, "coarse", swaps(COARSE, 1))
    inner2 = inner(SPLIT, 7 - SPLIT)
    edges = pl.pallas_call(
        x_edges_kernel,
        grid=(1,),
        in_specs=[
            plane(12, 0),
            plane(12, 7),
            plane(9, 7),
            pl.BlockSpec((1, 8, 256), lambda i: (7, 0, 0)),
            pl.BlockSpec((21, 8, 256), lambda i: (0, 0, 0)),
            pl.BlockSpec((21, 8, 256), lambda i: (0, 0, 0)),
            pl.BlockSpec((2, 192, 192), lambda i: (0, 0, 0)),
        ],
        out_specs=pl.BlockSpec((2, 12, 8, 256), lambda i: (0, 0, 0, 0)),
        out_shape=shape((2, 12, 8, 256), f32),
        scratch_shapes=[
            pltpu.VMEM((4, 4, 12, 8, 256), f32),
            pltpu.VMEM((2, 9, 8, 256), f32),
            pltpu.VMEM((8, 2, 192, 256), bf16),
        ],
        compiler_params=params(12),
        cost_estimate=cost(1.6),
        name="x_edges",
    )(loads, loads, rotations, occupancy, px1, px2, stiff)
    residual, coarse = pl.pallas_call(
        finish_kernel,
        in_specs=whole(12),
        out_specs=[pl.BlockSpec(memory_space=pltpu.MemorySpace.HBM)] + whole(1),
        out_shape=(shape((12, 8, 8, 256), f32), shape((256, 128), bf16)),
        scratch_shapes=[
            pltpu.VMEM((208, 256), f32),
            pltpu.VMEM((208, 256), f32),
            pltpu.VMEM((12, 8, 256), f32),
            pltpu.VMEM((12, 8, 256), f32),
            pltpu.VMEM((12, 8, 8, 256), f32),
            pltpu.VMEM((9, 2, 192, 256), bf16),
            pltpu.VMEM((2, 128, 256), f32),
            pltpu.SemaphoreType.DMA((12,)),
        ],
        compiler_params=params(16),
        name="finish",
    )(loads, first, last, py1, py2, near, far, stiff, table["lift"], inner1, inner2, edges)
    got = lax.all_to_all(coarse.reshape(32, 8, 128), "fine", 0, 0, tiled=True)
    sent = pl.pallas_call(
        lines_kernel,
        in_specs=whole(6),
        out_specs=whole(1)[0],
        out_shape=shape((256, 128), bf16),
        scratch_shapes=[
            pltpu.VMEM((256, 128), f32),
            pltpu.VMEM((256, 128), f32),
        ],
        compiler_params=params(16),
        name="lines",
    )(
        got.reshape(256, 128),
        line_inverse.reshape(16, 384, 384),
        *(table[k] for k in ("spread", "gather", "keep", "fold")),
    )
    back = lax.all_to_all(sent.reshape(32, 8, 128), "fine", 0, 0, tiled=True)
    displacement = pl.pallas_call(
        correct_kernel,
        in_specs=whole(4),
        out_specs=pl.BlockSpec(memory_space=pltpu.MemorySpace.HBM),
        out_shape=shape((12, 8, 8, 256), f32),
        scratch_shapes=[pltpu.VMEM((12, 8, 8, 256), f32), pltpu.SemaphoreType.DMA((12,))],
        compiler_params=params(12),
        name="correct",
    )(loads, back.reshape(256, 128), table["grown"], table["lift"])
    return displacement, residual


SPLIT = 4
FIRST = 8 << 20

def solution(mesh):
    in_specs = (
        P(None, "fine", "coarse", None),
        P(None, "fine", "coarse", None),
        P("fine", "coarse", None),
        P(),
        P("coarse", "fine", None, None),
    )
    out_specs = (P(None, "fine", "coarse", None), P(None, "fine", "coarse", None))
    return jax.shard_map(body, mesh=mesh, in_specs=in_specs, out_specs=out_specs, check_vma=False)
```

```python
import functools

import jax
import jax.numpy as jnp
import ml_dtypes
import numpy as np
from jax import lax
from jax.experimental import pallas as pl
from jax.experimental.pallas import tpu as pltpu
from jax.sharding import PartitionSpec as P

relax_step = 0.1
spring = 0.1
bf16 = jnp.bfloat16
f32 = jnp.float32
FINE = 32
COARSE = 4


def swaps(count, first):
    target = list(range(count))
    for i in range(first, count - 1, 2):
        target[i], target[i + 1] = i + 1, i
    return [(i, target[i]) for i in range(count)]


def tables():
    n = np.arange(384)
    n_i, n_f, n_x = n // 128, n % 128 // 4, n % 4
    r = np.arange(128)
    r_x, r_y = r % 16 // 8 * 2 + r % 2, r % 8 // 2
    slots = np.arange(32)
    rows = np.arange(256)
    z = np.arange(256)
    spread = n_f[:, None] == slots[None]
    keep, fold, lift = [], [], []
    for half in range(2):
        r_q = r // 16 + 6 * half
        keep.append((r[None] < 96) & (n_i[:, None] == r_q[None] // 4) & (n_x[:, None] == r_x[None]))
        for zz in range(4):
            to = r_y * 16 + zz * 4 + r_q % 4
            fold.append((r[:, None] < 96) & (to[:, None] == r[None]))
        mine = rows[:, None] % 8 // 4 == half
        lift.append(mine & (rows[:, None] // 8 * 4 + rows[:, None] % 4 == z[None] // 2))
    d_q, d_x, d_y = n // 32, n % 32 // 8, n % 8 // 2
    grown = (d_q[:, None] % 6 == r[None] // 16) & (d_x[:, None] == r_x[None]) & (d_y[:, None] == r_y[None])
    as_bf16 = lambda a: np.asarray(a, np.float32).astype(ml_dtypes.bfloat16)
    return {
        "spread": as_bf16(spread),
        "gather": as_bf16(spread.T),
        "keep": as_bf16(np.stack(keep)),
        "fold": as_bf16(np.stack(fold).reshape(4, 256, 128)),
        "lift": as_bf16(np.stack(lift)),
        "grown": as_bf16(grown),
    }


def rooted(occupancy):
    return jnp.sqrt(0.02 + 0.98 * occupancy.astype(f32))


def row_index():
    return lax.broadcasted_iota(jnp.int32, (8, 256), 0)


def next_z(v):
    lane = lax.broadcasted_iota(jnp.int32, v.shape, 1)
    return jnp.where(lane == 255, 0.0, pltpu.roll(v, 255, 1))


def past_z(v):
    lane = lax.broadcasted_iota(jnp.int32, v.shape, 1)
    return jnp.where(lane == 0, 0.0, pltpu.roll(v, 1, 1))


def x_faces_kernel(
    loads_ref, rot_ref, occ_ref, matrix_ref, one_ref, two_ref, loads_out, rot_out, occ_out, matrix_out, arrived
):
    face = [
        pltpu.make_async_copy(loads_ref.at[:, 0], loads_out.at[:, 0], arrived.at[0]),
        pltpu.make_async_copy(loads_ref.at[:, 7], loads_out.at[:, 7], arrived.at[1]),
        pltpu.make_async_copy(rot_ref.at[:, 7], rot_out.at[:, 7], arrived.at[2]),
        pltpu.make_async_copy(occ_ref, occ_out, arrived.at[3]),
    ]
    rest = [
        pltpu.make_async_copy(loads_ref.at[:, 1:7], loads_out.at[:, 1:7], arrived.at[4]),
        pltpu.make_async_copy(rot_ref.at[:, 0:7], rot_out.at[:, 0:7], arrived.at[5]),
        pltpu.make_async_copy(matrix_ref, matrix_out, arrived.at[6]),
    ]
    for copy in face + rest:
        copy.start()
    even = lax.axis_index("fine") % 2 == 0
    for copy in face:
        copy.wait()
    weight = rooted(occ_out[7])
    for q in range(12):
        low, high = loads_out[q, 0], loads_out[q, 7]
        one_ref[q] = jnp.where(even, high, low).astype(bf16)
        two_ref[q] = jnp.where(even, low, high).astype(bf16)
    for k in range(9):
        scaled = (rot_out[k, 7] * weight).astype(bf16)
        one_ref[12 + k] = scaled
        two_ref[12 + k] = scaled
    for copy in rest:
        copy.wait()


def x_sides(one_ref, two_ref, k):
    place = lax.axis_index("fine")
    even = place % 2 == 0
    one, two = one_ref[k].astype(f32), two_ref[k].astype(f32)
    low = jnp.where(place == 0, 0.0, jnp.where(even, two, one))
    high = jnp.where(place == FINE - 1, 0.0, jnp.where(even, one, two))
    return low, high


def rows_kernel(
    loads_ref, rot_ref, occ_ref, matrix_ref, first_ref, last_ref, stiff_ref, across_ref
):
    occ = [rooted(occ_ref[x]) for x in range(8)]
    for q in range(12):
        planes = [loads_ref[q, x] for x in range(8)]
        first_ref[q] = jnp.concatenate([p[0:1] for p in planes], 0)
        last_ref[q] = jnp.concatenate([p[7:8] for p in planes], 0)
    for k in range(9):
        planes = [rot_ref[k, x] * occ[x] for x in range(8)]
        last_ref[12 + k] = jnp.concatenate([p[7:8] for p in planes], 0)
    block = lax.broadcasted_iota(jnp.int32, (192, 24), 0) >> 3
    place = (block * 11) >> 5
    corner = (place & 3) + (place & 2) + (place >> 2) * 2
    part = block - 3 * place
    copy = (corner * 3 + part == lax.broadcasted_iota(jnp.int32, (192, 24), 1)).astype(bf16)

    def same(size):
        row = lax.broadcasted_iota(jnp.int32, (size, size), 0)
        return ((row ^ lax.broadcasted_iota(jnp.int32, (size, size), 1)) & 7) == 0

    whole_matrix = matrix_ref[...]
    main = whole_matrix.astype(bf16)
    rest = (whole_matrix - main.astype(f32)).astype(bf16)
    for slot, part in ((0, main), (1, rest)):
        wide = jnp.dot(copy, part, preferred_element_type=f32).astype(bf16)
        nt = (((1,), (1,)), ((), ()))
        full = lax.dot_general(wide, copy, nt, preferred_element_type=f32)
        stiff_ref[slot] = jnp.where(same(192), full, 0.0).astype(bf16)
        full = lax.dot_general(wide[0:96], copy[96:192], nt, preferred_element_type=f32)
        across_ref[slot] = jnp.where(same(96), full, 0.0).astype(bf16)


def y_faces_kernel(first_ref, last_ref, px1_ref, px2_ref, one_ref, two_ref, near_ref, far_ref):
    even = lax.axis_index("coarse") % 2 == 0
    sides = [x_sides(px1_ref, px2_ref, k) for k in range(21)]

    def column(side, count, row, rows):
        picked = [sides[k][side][row : row + 1] for k in range(count)]
        return jnp.concatenate(picked + [jnp.zeros((rows - count, 256), f32)], 0)

    def send(tile, last, first):
        one_ref[tile] = jnp.where(even, last, first).astype(bf16)
        two_ref[tile] = jnp.where(even, first, last).astype(bf16)

    for k in range(21):
        last = last_ref[k]
        send(k, last, first_ref[k] if k < 12 else last)
    low_last = column(0, 21, 7, 24)
    near_low, high_last, near_high = column(0, 12, 0, 16), column(1, 12, 7, 16), column(1, 12, 0, 16)
    near_ref[0] = near_low
    near_ref[1] = near_high
    far_ref[...] = low_last[8:24]
    for tile in range(2):
        at = 8 * tile
        send(21 + tile, low_last[at : at + 8], near_low[at : at + 8])
        send(24 + tile, high_last[at : at + 8], near_high[at : at + 8])
    send(23, low_last[16:24], low_last[16:24])


def turn_in(scale, nodes):
    return [
        scale[i] * nodes[0] + scale[3 + i] * nodes[1] + scale[6 + i] * nodes[2] for i in range(3)
    ]


def turn_out(scale, forces):
    return [
        scale[3 * i] * forces[0] + scale[3 * i + 1] * forces[1] + scale[3 * i + 2] * forces[2]
        for i in range(3)
    ]


ORDER = (0, 1, 4, 5, 2, 3, 6, 7)


def element_forces(main, rest, local, scale, pick, corners=ORDER):
    held, at = [], 0
    for corner in corners:
        held += turn_in(scale, pick(corner))
        while len(held) >= 2:
            pair = jnp.concatenate(held[:2], 0)
            upper = pair.astype(bf16)
            local[0, 16 * at : 16 * at + 16] = upper
            local[1, 16 * at : 16 * at + 16] = (pair - upper.astype(f32)).astype(bf16)
            held, at = held[2:], at + 1
    used = 16 * at
    out = jnp.dot(main, local[0, 0:used], preferred_element_type=f32)
    out = out + jnp.dot(rest, local[0, 0:used], preferred_element_type=f32)
    return out + jnp.dot(main, local[1, 0:used], preferred_element_type=f32)


def in_turn(steps):
    held = None
    for make, use in steps:
        out = make()
        if held is not None:
            held[0](held[1])
        held = (use, out)
    held[0](held[1])


def corner_rows(out, corner, skipped=0):
    at = 24 * (ORDER.index(corner) - skipped)
    return [out[at + 8 * j : at + 8 * j + 8] for j in range(3)]


def put_nodes(nodes, p, q, v):
    up = jnp.where(row_index() == 7, 0.0, pltpu.roll(v, 7, 0))
    nodes[p, 0, q] = v
    nodes[p, 1, q] = up
    nodes[p, 2, q] = next_z(v)
    nodes[p, 3, q] = next_z(up)


def settle(sides):
    own = sides[0] + past_z(sides[2])
    upper = sides[1] + past_z(sides[3])
    return own + jnp.where(row_index() == 0, 0.0, pltpu.roll(upper, 1, 0))


def picker(nodes, p, case):
    def pick(corner):
        off_x, off_y, off_z = corner % 2, corner // 2 % 2, corner // 4
        return [nodes[p + off_x, off_y + 2 * off_z, j * 4 + case] for j in range(3)]

    return pick


def inner_kernel(start, count, loads_ref, rot_ref, occ_ref, stiff_ref, force_ref, nodes, carry, local):
    for p in range(count + 1):
        for q in range(12):
            put_nodes(nodes, p, q, loads_ref[q, start + p])
    steps = []
    for e in range(count):
        weight = rooted(occ_ref[start + e])
        turns = [rot_ref[k, start + e] * weight for k in range(9)]

        def make(case, e=e, scale=turns):
            pick = picker(nodes, e, case)
            return element_forces(stiff_ref[0], stiff_ref[1], local.at[4 * e + case], scale, pick)

        def use(case, out, e=e, scale=turns):
            total = [[None] * 4 for _ in range(3)]
            for corner in range(8):
                turned = turn_out(scale, corner_rows(out, corner))
                for i in range(3):
                    q = i * 4 + case
                    if corner % 2 == 0:
                        past = carry[e, corner // 2, q] if e else 0.0
                        total[i][corner // 2] = turned[i] + past
                    else:
                        carry[e + 1, corner // 2, q] = turned[i]
            for i in range(3):
                force_ref[i * 4 + case, e] = settle(total[i])

        steps += [(functools.partial(make, k), functools.partial(use, k)) for k in range(4)]
    in_turn(steps)
    for q in range(12):
        force_ref[q, count] = settle([carry[count, side, q] for side in range(4)])


def x_edges_kernel(
    low_ref, high_ref, rot_ref, occ_ref, px1_ref, px2_ref, stiff_ref, force_ref, nodes, scales, local
):
    weight = rooted(occ_ref[0])
    for q in range(12):
        low, high = x_sides(px1_ref, px2_ref, q)
        for p, v in enumerate((low, low_ref[q, 0], high_ref[q, 0], high)):
            put_nodes(nodes, p, q, v)
    for k in range(9):
        low, _ = x_sides(px1_ref, px2_ref, 12 + k)
        scales[0, k] = low
        scales[1, k] = rot_ref[k, 0] * weight
    def make(edge, case):
        scale = [scales[edge, k] for k in range(9)]
        pick = picker(nodes, 2 * edge, case)
        return element_forces(stiff_ref[0], stiff_ref[1], local.at[4 * edge + case], scale, pick)

    def use(edge, case, out):
        scale = [scales[edge, k] for k in range(9)]
        sides = [turn_out(scale, corner_rows(out, 2 * side + 1 - edge)) for side in range(4)]
        for i in range(3):
            force_ref[edge, i * 4 + case] = settle([side[i] for side in sides])

    steps = [(edge, case) for edge in range(2) for case in range(4)]
    in_turn([(functools.partial(make, *k), functools.partial(use, *k)) for k in steps])


def finish_kernel(
    loads_ref,
    first_ref,
    last_ref,
    py1_ref,
    py2_ref,
    near_ref,
    far_ref,
    stiff_ref,
    across_ref,
    lift_ref,
    inner1_ref,
    inner2_ref,
    edges_ref,
    residual_ref,
    coarse_ref,
    below,
    above,
    low,
    high,
    local,
    sums,
):
    row = row_index()
    place = lax.axis_index("coarse")
    even = place % 2 == 0
    for k in range(26):
        one, two = py1_ref[k].astype(f32), py2_ref[k].astype(f32)
        below[8 * k : 8 * k + 8] = jnp.where(place == 0, 0.0, jnp.where(even, two, one))
        above[8 * k : 8 * k + 8] = jnp.where(place == COARSE - 1, 0.0, jnp.where(even, one, two))

    def tile(source, k):
        return source[8 * k : 8 * k + 8]

    def single(source, at):
        return source[at : at + 1]

    lower = row < 4
    scale = [jnp.where(lower, single(below, 180 + k), single(far_ref, 4 + k)) for k in range(9)]

    def pick_first(corner):
        off_x, off_y, off_z = corner % 2, corner // 2 % 2, corner // 4
        got = []
        for j in range(3):
            rows = []
            for case in range(4):
                q = j * 4 + case
                if off_y:
                    rows.append(first_ref[q, 0:1] if off_x else near_ref[0, q : q + 1])
                else:
                    rows.append(single(below, 8 * q if off_x else 168 + q))
            if off_y:
                rows += [single(above, 8 * q if off_x else 168 + q) for q in range(4 * j, 4 * j + 4)]
            else:
                rows.append(jnp.zeros((4, 256), f32))
            got.append(jnp.concatenate(rows, 0))
        return [next_z(v) for v in got] if off_z else got

    ends = []

    def make_first():
        return element_forces(stiff_ref[0], stiff_ref[1], local.at[8], scale, pick_first)

    def use_first(out):
        flat = [jnp.where(lower, u, v) for u, v in zip(corner_rows(out, 3), corner_rows(out, 1))]
        tall = [jnp.where(lower, u, v) for u, v in zip(corner_rows(out, 7), corner_rows(out, 5))]
        flat, tall = turn_out(scale, flat), turn_out(scale, tall)
        ends.extend(flat[i] + past_z(tall[i]) for i in range(3))

    steps = [(make_first, use_first)]
    for upper in range(2):
        turns = [last_ref[12 + k] if upper else tile(below, 12 + k) for k in range(9)]
        for case in range(4):

            def pick(corner, upper=upper, case=case):
                off_x, off_y, off_z = corner % 2, corner // 2 % 2, corner // 4
                got = []
                for q in (case, 4 + case, 8 + case):
                    if not upper and off_y:
                        v, past = first_ref[q], near_ref[1, q : q + 1]
                    else:
                        source = above if upper else below
                        v, past = tile(source, q), single(source, 192 + q)
                    got.append(jnp.where(row == 7, past, pltpu.roll(v, 7, 0)) if off_x else v)
                return [next_z(v) for v in got] if off_z else got

            def make(upper=upper, case=case, turns=turns, pick=pick):
                slot = local.at[4 * upper + case]
                if upper:
                    return element_forces(across_ref[0], across_ref[1], slot, turns, pick, ORDER[4:])
                return element_forces(stiff_ref[0, 96:192], stiff_ref[1, 96:192], slot, turns, pick)

            def use(out, upper=upper, case=case, turns=turns):
                skipped = 0 if upper else 4
                sides = []
                for off_x in range(2):
                    flat = turn_out(turns, corner_rows(out, off_x + 2 - 2 * upper, skipped))
                    tall = turn_out(turns, corner_rows(out, off_x + 6 - 2 * upper, skipped))
                    sides.append([flat[i] + past_z(tall[i]) for i in range(3)])
                at = 4 * upper + case
                for i in range(3):
                    past = jnp.where(row == 0, ends[i][at : at + 1], pltpu.roll(sides[1][i], 1, 0))
                    (low, high)[upper][i * 4 + case] = sides[0][i] + past

            steps.append((make, use))
    in_turn(steps)

    def residual_of(q, x, force):
        force = force + jnp.where(row == 0, low[q, x : x + 1], 0.0)
        force = force + jnp.where(row == 7, high[q, x : x + 1], 0.0)
        given = loads_ref[q, x]
        left = given - relax_step * (spring * given + force)
        residual_ref[q, x] = left
        return left

    split = inner1_ref.shape[1] - 1
    for q in range(12):
        planes = []
        for x in range(8):
            force = inner1_ref[q, x] if x <= split else inner2_ref[q, x - split]
            if x == split:
                force = force + inner2_ref[q, 0]
            if x in (0, 7):
                force = force + edges_ref[x // 7, q]
            planes.append(residual_of(q, x, force))
        for half in range(2):
            s0 = planes[4 * half] + planes[4 * half + 1]
            s1 = planes[4 * half + 2] + planes[4 * half + 3]
            t0 = s0 + pltpu.roll(s0, 7, 0)
            t1 = s1 + pltpu.roll(s1, 1, 0)
            at = 16 * (q % 6) + 8 * half
            sums[q // 6, at : at + 8] = jnp.where(row % 2 == 0, t0, t1)
    nt = (((1,), (1,)), ((), ()))
    coarse = None
    for half in range(2):
        sums[half, 96:128] = jnp.zeros((32, 256), f32)
        every = sums[half]
        main = every.astype(bf16)
        rest = (every - main.astype(f32)).astype(bf16)
        for part in (main, rest):
            term = lax.dot_general(lift_ref[half], part, nt, preferred_element_type=f32)
            coarse = term if coarse is None else coarse + term
    coarse_ref[...] = coarse.astype(bf16)


def lines_kernel(
    got_ref,
    inverse_ref,
    spread_ref,
    gather_ref,
    keep_ref,
    fold_ref,
    made_ref,
    sent_ref,
    residual_ref,
    rows,
    back,
    stored,
):
    store = pltpu.make_async_copy(made_ref, residual_ref, stored)
    store.start()
    nt = (((1,), (1,)), ((), ()))
    rows[...] = got_ref[...].astype(f32)
    vectors = jnp.zeros((384, 128), f32)
    for half in range(2):
        keep = keep_ref[half].astype(f32)
        keep = jnp.concatenate([keep, keep], 1)
        for pair in range(2 * half, 2 * half + 2):
            part = [rows[pl.ds(2 * pair + k, 32, stride=8), :] for k in range(2)]
            part = jnp.concatenate(part, 1).astype(bf16)
            wide = jnp.dot(spread_ref[...], part, preferred_element_type=f32) * keep
            vectors = vectors + jnp.dot(wide.astype(bf16), fold_ref[pair], preferred_element_type=f32)
    vectors = vectors.astype(bf16)
    line = lax.broadcasted_iota(jnp.int32, (384, 128), 1) // 4
    solved = jnp.zeros((384, 128), f32)
    for k in range(16):
        one = jnp.dot(inverse_ref[k], vectors, preferred_element_type=f32)
        solved = jnp.where(line == k, one, solved)
    solved = solved.astype(bf16)
    for half in range(2):
        keep = keep_ref[half].astype(f32)
        keep = jnp.concatenate([keep, keep], 1)
        for pair in range(2 * half, 2 * half + 2):
            wide = lax.dot_general(solved, fold_ref[pair], nt, preferred_element_type=f32) * keep
            part = jnp.dot(gather_ref[...], wide.astype(bf16), preferred_element_type=f32)
            for k in range(2):
                back[pl.ds(2 * pair + k, 32, stride=8), :] = part[:, 128 * k : 128 * k + 128]
    sent_ref[...] = back[...].astype(bf16)
    store.wait()


def correct_kernel(loads_ref, back_ref, grown_ref, lift_ref, out_ref, made, sent):
    nt = (((1,), (1,)), ((), ()))
    copies = [pltpu.make_async_copy(made.at[q], out_ref.at[q], sent.at[q]) for q in range(12)]
    for half in range(2):
        mine = grown_ref[192 * half : 192 * half + 192]
        mine = lax.dot_general(mine, back_ref[...], nt, preferred_element_type=f32)
        coarse = jnp.dot(mine.astype(bf16), lift_ref[half], preferred_element_type=f32)
        for q in range(6 * half, 6 * half + 6):
            for part in range(4):
                at = 32 * (q % 6) + 8 * part
                added = coarse[at : at + 8]
                for x in (2 * part, 2 * part + 1):
                    made[q, x] = relax_step * loads_ref[q, x] + added
            copies[q].start()
    for copy in copies:
        copy.wait()


def whole(count):
    return [pl.BlockSpec(memory_space=pltpu.VMEM)] * count


def params(mib):
    return pltpu.CompilerParams(vmem_limit_bytes=mib << 20)


def cost(us):
    return pl.CostEstimate(flops=0, bytes_accessed=int(us * 3.0e6), transcendentals=0)


def body(loads, rotations, occupancy, element_matrix, line_inverse):
    table = {name: jnp.asarray(value) for name, value in tables().items()}
    shape = jax.ShapeDtypeStruct
    face = shape((21, 8, 256), bf16)
    plane = lambda count, at: pl.BlockSpec((count, 1, 8, 256), lambda i: (0, at, 0, 0))
    px1, px2, loads, rotations, occupancy, matrix = pl.pallas_call(
        x_faces_kernel,
        in_specs=[pl.BlockSpec(memory_space=pltpu.MemorySpace.HBM)] * 4,
        out_specs=whole(6),
        out_shape=(
            face,
            face,
            shape(loads.shape, f32),
            shape(rotations.shape, f32),
            shape(occupancy.shape, jnp.int32),
            shape((24, 24), f32),
        ),
        scratch_shapes=[pltpu.SemaphoreType.DMA((7,))],
        compiler_params=pltpu.CompilerParams(vmem_limit_bytes=FIRST),
        name="x_faces",
    )(*(pltpu.with_memory_space_constraint(a, pltpu.MemorySpace.HBM) for a in (loads, rotations, occupancy, element_matrix)))
    px1 = lax.ppermute(px1, "fine", swaps(FINE, 0))
    px2 = lax.ppermute(px2, "fine", swaps(FINE, 1))
    first, last, stiff, across = pl.pallas_call(
        rows_kernel,
        in_specs=whole(4),
        out_specs=whole(4),
        out_shape=(shape((12, 8, 256), f32), shape((21, 8, 256), f32), shape((2, 192, 192), bf16), shape((2, 96, 96), bf16)),
        compiler_params=params(8),
        cost_estimate=cost(2),
        name="rows",
    )(loads, rotations, occupancy, matrix)

    def inner(start, count):
        return pl.pallas_call(
            functools.partial(inner_kernel, start, count),
            in_specs=whole(4),
            out_specs=whole(1)[0],
            out_shape=shape((12, count + 1, 8, 256), f32),
            scratch_shapes=[
                pltpu.VMEM((count + 1, 4, 12, 8, 256), f32),
                pltpu.VMEM((count + 1, 4, 12, 8, 256), f32),
                pltpu.VMEM((4 * count, 2, 192, 256), bf16),
            ],
            compiler_params=params(20),
            cost_estimate=cost(0.8 * count),
            name=f"inner_{start}",
        )(loads, rotations, occupancy, stiff)

    inner1 = inner(0, SPLIT)
    first, inner1 = lax.optimization_barrier((first, inner1))
    face = shape((26, 8, 256), bf16)
    py1, py2, near, far = pl.pallas_call(
        y_faces_kernel,
        in_specs=whole(4),
        out_specs=whole(4),
        out_shape=(face, face, shape((2, 16, 256), f32), shape((16, 256), f32)),
        compiler_params=params(8),
        name="y_faces",
    )(first, last, px1, px2)
    py1 = lax.ppermute(py1, "coarse", swaps(COARSE, 0))
    py2 = lax.ppermute(py2, "coarse", swaps(COARSE, 1))
    inner2 = inner(SPLIT, 7 - SPLIT)
    edges = pl.pallas_call(
        x_edges_kernel,
        grid=(1,),
        in_specs=[
            plane(12, 0),
            plane(12, 7),
            plane(9, 7),
            pl.BlockSpec((1, 8, 256), lambda i: (7, 0, 0)),
            pl.BlockSpec((21, 8, 256), lambda i: (0, 0, 0)),
            pl.BlockSpec((21, 8, 256), lambda i: (0, 0, 0)),
            pl.BlockSpec((2, 192, 192), lambda i: (0, 0, 0)),
        ],
        out_specs=pl.BlockSpec((2, 12, 8, 256), lambda i: (0, 0, 0, 0)),
        out_shape=shape((2, 12, 8, 256), f32),
        scratch_shapes=[
            pltpu.VMEM((4, 4, 12, 8, 256), f32),
            pltpu.VMEM((2, 9, 8, 256), f32),
            pltpu.VMEM((8, 2, 192, 256), bf16),
        ],
        compiler_params=params(12),
        cost_estimate=cost(1.6),
        name="x_edges",
    )(loads, loads, rotations, occupancy, px1, px2, stiff)
    residual, coarse = pl.pallas_call(
        finish_kernel,
        in_specs=whole(13),
        out_specs=whole(2),
        out_shape=(shape((12, 8, 8, 256), f32), shape((256, 128), bf16)),
        scratch_shapes=[
            pltpu.VMEM((208, 256), f32),
            pltpu.VMEM((208, 256), f32),
            pltpu.VMEM((12, 8, 256), f32),
            pltpu.VMEM((12, 8, 256), f32),
            pltpu.VMEM((9, 2, 192, 256), bf16),
            pltpu.VMEM((2, 128, 256), f32),
        ],
        compiler_params=params(16),
        name="finish",
    )(loads, first, last, py1, py2, near, far, stiff, across, table["lift"], inner1, inner2, edges)
    got = lax.all_to_all(coarse.reshape(32, 8, 128), "fine", 0, 0, tiled=True)
    sent, residual = pl.pallas_call(
        lines_kernel,
        in_specs=whole(7),
        out_specs=whole(1) + [pl.BlockSpec(memory_space=pltpu.MemorySpace.HBM)],
        out_shape=(shape((256, 128), bf16), shape((12, 8, 8, 256), f32)),
        scratch_shapes=[
            pltpu.VMEM((256, 128), f32),
            pltpu.VMEM((256, 128), f32),
            pltpu.SemaphoreType.DMA,
        ],
        compiler_params=params(16),
        name="lines",
    )(
        got.reshape(256, 128),
        line_inverse.reshape(16, 384, 384),
        *(table[k] for k in ("spread", "gather", "keep", "fold")),
        residual,
    )
    back = lax.all_to_all(sent.reshape(32, 8, 128), "fine", 0, 0, tiled=True)
    displacement = pl.pallas_call(
        correct_kernel,
        in_specs=whole(4),
        out_specs=pl.BlockSpec(memory_space=pltpu.MemorySpace.HBM),
        out_shape=shape((12, 8, 8, 256), f32),
        scratch_shapes=[pltpu.VMEM((12, 8, 8, 256), f32), pltpu.SemaphoreType.DMA((12,))],
        compiler_params=params(12),
        name="correct",
    )(loads, back.reshape(256, 128), table["grown"], table["lift"])
    return displacement, residual


SPLIT = 5
FIRST = 8 << 20

def solution(mesh):
    in_specs = (
        P(None, "fine", "coarse", None),
        P(None, "fine", "coarse", None),
        P("fine", "coarse", None),
        P(),
        P("coarse", "fine", None, None),
    )
    out_specs = (P(None, "fine", "coarse", None), P(None, "fine", "coarse", None))
    return jax.shard_map(body, mesh=mesh, in_specs=in_specs, out_specs=out_specs, check_vma=False)
```

```python
import functools

import jax
import jax.numpy as jnp
import ml_dtypes
import numpy as np
from jax import lax
from jax.experimental import pallas as pl
from jax.experimental.pallas import tpu as pltpu
from jax.sharding import PartitionSpec as P

relax_step = 0.1
spring = 0.1
bf16 = jnp.bfloat16
f32 = jnp.float32
FINE = 32
COARSE = 4


def swaps(count, first):
    target = list(range(count))
    for i in range(first, count - 1, 2):
        target[i], target[i + 1] = i + 1, i
    return [(i, target[i]) for i in range(count)]


def tables():
    n = np.arange(384)
    n_i, n_f, n_x = n // 128, n % 128 // 4, n % 4
    r = np.arange(128)
    r_x, r_y = r % 16 // 8 * 2 + r % 2, r % 8 // 2
    slots = np.arange(32)
    rows = np.arange(256)
    z = np.arange(256)
    spread = n_f[:, None] == slots[None]
    keep, fold, lift = [], [], []
    for half in range(2):
        r_q = r // 16 + 6 * half
        keep.append((r[None] < 96) & (n_i[:, None] == r_q[None] // 4) & (n_x[:, None] == r_x[None]))
        for zz in range(4):
            to = r_y * 16 + zz * 4 + r_q % 4
            fold.append((r[:, None] < 96) & (to[:, None] == r[None]))
        mine = rows[:, None] % 8 // 4 == half
        lift.append(mine & (rows[:, None] // 8 * 4 + rows[:, None] % 4 == z[None] // 2))
    d_q, d_x, d_y = n // 32, n % 32 // 8, n % 8 // 2
    grown = (d_q[:, None] % 6 == r[None] // 16) & (d_x[:, None] == r_x[None]) & (d_y[:, None] == r_y[None])
    as_bf16 = lambda a: np.asarray(a, np.float32).astype(ml_dtypes.bfloat16)
    return {
        "spread": as_bf16(spread),
        "gather": as_bf16(spread.T),
        "keep": as_bf16(np.stack(keep)),
        "fold": as_bf16(np.stack(fold).reshape(4, 256, 128)),
        "lift": as_bf16(np.stack(lift)),
        "grown": as_bf16(grown),
    }


def rooted(occupancy):
    return jnp.sqrt(0.02 + 0.98 * occupancy.astype(f32))


def row_index():
    return lax.broadcasted_iota(jnp.int32, (8, 256), 0)


def next_z(v):
    lane = lax.broadcasted_iota(jnp.int32, v.shape, 1)
    return jnp.where(lane == 255, 0.0, pltpu.roll(v, 255, 1))


def past_z(v):
    lane = lax.broadcasted_iota(jnp.int32, v.shape, 1)
    return jnp.where(lane == 0, 0.0, pltpu.roll(v, 1, 1))


def x_faces_kernel(
    loads_ref, rot_ref, occ_ref, matrix_ref, one_ref, two_ref, matrix_out, faces, turns, bone, arrived
):
    copies = [
        pltpu.make_async_copy(loads_ref.at[:, 0], faces.at[0], arrived.at[0]),
        pltpu.make_async_copy(loads_ref.at[:, 7], faces.at[1], arrived.at[1]),
        pltpu.make_async_copy(rot_ref.at[:, 7], turns, arrived.at[2]),
        pltpu.make_async_copy(occ_ref.at[7], bone, arrived.at[3]),
        pltpu.make_async_copy(matrix_ref, matrix_out, arrived.at[4]),
    ]
    for copy in copies:
        copy.start()
    even = lax.axis_index("fine") % 2 == 0
    for copy in copies:
        copy.wait()
    weight = rooted(bone[...])
    for q in range(12):
        low, high = faces[0, q], faces[1, q]
        one_ref[q] = jnp.where(even, high, low).astype(bf16)
        two_ref[q] = jnp.where(even, low, high).astype(bf16)
    for k in range(9):
        scaled = (turns[k] * weight).astype(bf16)
        one_ref[12 + k] = scaled
        two_ref[12 + k] = scaled


def x_sides(one_ref, two_ref, k):
    place = lax.axis_index("fine")
    even = place % 2 == 0
    one, two = one_ref[k].astype(f32), two_ref[k].astype(f32)
    low = jnp.where(place == 0, 0.0, jnp.where(even, two, one))
    high = jnp.where(place == FINE - 1, 0.0, jnp.where(even, one, two))
    return low, high


def rows_kernel(
    loads_hbm,
    rot_hbm,
    occ_hbm,
    matrix_ref,
    loads_ref,
    rot_ref,
    occ_ref,
    first_ref,
    last_ref,
    stiff_ref,
    across_ref,
    arrived,
):
    copies = [
        pltpu.make_async_copy(loads_hbm, loads_ref, arrived.at[0]),
        pltpu.make_async_copy(rot_hbm, rot_ref, arrived.at[1]),
        pltpu.make_async_copy(occ_hbm, occ_ref, arrived.at[2]),
    ]
    for copy in copies:
        copy.start()
    block = lax.broadcasted_iota(jnp.int32, (192, 24), 0) >> 3
    place = (block * 11) >> 5
    corner = (place & 3) + (place & 2) + (place >> 2) * 2
    part = block - 3 * place
    copy = (corner * 3 + part == lax.broadcasted_iota(jnp.int32, (192, 24), 1)).astype(bf16)

    def same(size):
        row = lax.broadcasted_iota(jnp.int32, (size, size), 0)
        return ((row ^ lax.broadcasted_iota(jnp.int32, (size, size), 1)) & 7) == 0

    whole_matrix = matrix_ref[...]
    main = whole_matrix.astype(bf16)
    rest = (whole_matrix - main.astype(f32)).astype(bf16)
    for slot, part in ((0, main), (1, rest)):
        wide = jnp.dot(copy, part, preferred_element_type=f32).astype(bf16)
        nt = (((1,), (1,)), ((), ()))
        full = lax.dot_general(wide, copy, nt, preferred_element_type=f32)
        stiff_ref[slot] = jnp.where(same(192), full, 0.0).astype(bf16)
        full = lax.dot_general(wide[0:96], copy[96:192], nt, preferred_element_type=f32)
        across_ref[slot] = jnp.where(same(96), full, 0.0).astype(bf16)
    for copy in copies:
        copy.wait()
    occ = [rooted(occ_ref[x]) for x in range(8)]
    for q in range(12):
        planes = [loads_ref[q, x] for x in range(8)]
        first_ref[q] = jnp.concatenate([p[0:1] for p in planes], 0)
        last_ref[q] = jnp.concatenate([p[7:8] for p in planes], 0)
    for k in range(9):
        planes = [rot_ref[k, x] * occ[x] for x in range(8)]
        last_ref[12 + k] = jnp.concatenate([p[7:8] for p in planes], 0)


def y_faces_kernel(first_ref, last_ref, px1_ref, px2_ref, one_ref, two_ref, near_ref, far_ref):
    even = lax.axis_index("coarse") % 2 == 0
    sides = [x_sides(px1_ref, px2_ref, k) for k in range(21)]

    def column(side, count, row, rows):
        picked = [sides[k][side][row : row + 1] for k in range(count)]
        return jnp.concatenate(picked + [jnp.zeros((rows - count, 256), f32)], 0)

    def send(tile, last, first):
        one_ref[tile] = jnp.where(even, last, first).astype(bf16)
        two_ref[tile] = jnp.where(even, first, last).astype(bf16)

    for k in range(21):
        last = last_ref[k]
        send(k, last, first_ref[k] if k < 12 else last)
    low_last = column(0, 21, 7, 24)
    near_low, high_last, near_high = column(0, 12, 0, 16), column(1, 12, 7, 16), column(1, 12, 0, 16)
    near_ref[0] = near_low
    near_ref[1] = near_high
    far_ref[...] = low_last[8:24]
    for tile in range(2):
        at = 8 * tile
        send(21 + tile, low_last[at : at + 8], near_low[at : at + 8])
        send(24 + tile, high_last[at : at + 8], near_high[at : at + 8])
    send(23, low_last[16:24], low_last[16:24])


def turn_in(scale, nodes):
    return [
        scale[i] * nodes[0] + scale[3 + i] * nodes[1] + scale[6 + i] * nodes[2] for i in range(3)
    ]


def turn_out(scale, forces):
    return [
        scale[3 * i] * forces[0] + scale[3 * i + 1] * forces[1] + scale[3 * i + 2] * forces[2]
        for i in range(3)
    ]


ORDER = (0, 1, 4, 5, 2, 3, 6, 7)


def element_forces(main, rest, local, scale, pick, corners=ORDER):
    held, at = [], 0
    for corner in corners:
        held += turn_in(scale, pick(corner))
        while len(held) >= 2:
            pair = jnp.concatenate(held[:2], 0)
            upper = pair.astype(bf16)
            local[0, 16 * at : 16 * at + 16] = upper
            local[1, 16 * at : 16 * at + 16] = (pair - upper.astype(f32)).astype(bf16)
            held, at = held[2:], at + 1
    used = 16 * at
    out = jnp.dot(main, local[0, 0:used], preferred_element_type=f32)
    out = out + jnp.dot(rest, local[0, 0:used], preferred_element_type=f32)
    return out + jnp.dot(main, local[1, 0:used], preferred_element_type=f32)


def in_turn(steps):
    held = None
    for make, use in steps:
        out = make()
        if held is not None:
            held[0](held[1])
        held = (use, out)
    held[0](held[1])


def corner_rows(out, corner, skipped=0):
    at = 24 * (ORDER.index(corner) - skipped)
    return [out[at + 8 * j : at + 8 * j + 8] for j in range(3)]


def put_nodes(nodes, p, q, v):
    up = jnp.where(row_index() == 7, 0.0, pltpu.roll(v, 7, 0))
    nodes[p, 0, q] = v
    nodes[p, 1, q] = up
    nodes[p, 2, q] = next_z(v)
    nodes[p, 3, q] = next_z(up)


def settle(sides):
    own = sides[0] + past_z(sides[2])
    upper = sides[1] + past_z(sides[3])
    return own + jnp.where(row_index() == 0, 0.0, pltpu.roll(upper, 1, 0))


def picker(nodes, p, case):
    def pick(corner):
        off_x, off_y, off_z = corner % 2, corner // 2 % 2, corner // 4
        return [nodes[p + off_x, off_y + 2 * off_z, j * 4 + case] for j in range(3)]

    return pick


def inner_kernel(start, count, loads_ref, rot_ref, occ_ref, stiff_ref, force_ref, nodes, carry, local):
    for p in range(count + 1):
        for q in range(12):
            put_nodes(nodes, p, q, loads_ref[q, start + p])
    steps = []
    for e in range(count):
        weight = rooted(occ_ref[start + e])
        turns = [rot_ref[k, start + e] * weight for k in range(9)]

        def make(case, e=e, scale=turns):
            pick = picker(nodes, e, case)
            return element_forces(stiff_ref[0], stiff_ref[1], local.at[4 * e + case], scale, pick)

        def use(case, out, e=e, scale=turns):
            total = [[None] * 4 for _ in range(3)]
            for corner in range(8):
                turned = turn_out(scale, corner_rows(out, corner))
                for i in range(3):
                    q = i * 4 + case
                    if corner % 2 == 0:
                        past = carry[e, corner // 2, q] if e else 0.0
                        total[i][corner // 2] = turned[i] + past
                    else:
                        carry[e + 1, corner // 2, q] = turned[i]
            for i in range(3):
                force_ref[i * 4 + case, e] = settle(total[i])

        steps += [(functools.partial(make, k), functools.partial(use, k)) for k in range(4)]
    in_turn(steps)
    for q in range(12):
        force_ref[q, count] = settle([carry[count, side, q] for side in range(4)])


def x_edges_kernel(
    low_ref, high_ref, rot_ref, occ_ref, px1_ref, px2_ref, stiff_ref, force_ref, nodes, scales, local
):
    weight = rooted(occ_ref[0])
    for q in range(12):
        low, high = x_sides(px1_ref, px2_ref, q)
        for p, v in enumerate((low, low_ref[q, 0], high_ref[q, 0], high)):
            put_nodes(nodes, p, q, v)
    for k in range(9):
        low, _ = x_sides(px1_ref, px2_ref, 12 + k)
        scales[0, k] = low
        scales[1, k] = rot_ref[k, 0] * weight
    def make(edge, case):
        scale = [scales[edge, k] for k in range(9)]
        pick = picker(nodes, 2 * edge, case)
        return element_forces(stiff_ref[0], stiff_ref[1], local.at[4 * edge + case], scale, pick)

    def use(edge, case, out):
        scale = [scales[edge, k] for k in range(9)]
        sides = [turn_out(scale, corner_rows(out, 2 * side + 1 - edge)) for side in range(4)]
        for i in range(3):
            force_ref[edge, i * 4 + case] = settle([side[i] for side in sides])

    steps = [(edge, case) for edge in range(2) for case in range(4)]
    in_turn([(functools.partial(make, *k), functools.partial(use, *k)) for k in steps])


def finish_kernel(
    loads_ref,
    first_ref,
    last_ref,
    py1_ref,
    py2_ref,
    near_ref,
    far_ref,
    stiff_ref,
    across_ref,
    lift_ref,
    inner1_ref,
    inner2_ref,
    edges_ref,
    residual_ref,
    coarse_ref,
    below,
    above,
    low,
    high,
    local,
    sums,
):
    row = row_index()
    place = lax.axis_index("coarse")
    even = place % 2 == 0
    for k in range(26):
        one, two = py1_ref[k].astype(f32), py2_ref[k].astype(f32)
        below[8 * k : 8 * k + 8] = jnp.where(place == 0, 0.0, jnp.where(even, two, one))
        above[8 * k : 8 * k + 8] = jnp.where(place == COARSE - 1, 0.0, jnp.where(even, one, two))

    def tile(source, k):
        return source[8 * k : 8 * k + 8]

    def single(source, at):
        return source[at : at + 1]

    lower = row < 4
    scale = [jnp.where(lower, single(below, 180 + k), single(far_ref, 4 + k)) for k in range(9)]

    def pick_first(corner):
        off_x, off_y, off_z = corner % 2, corner // 2 % 2, corner // 4
        got = []
        for j in range(3):
            rows = []
            for case in range(4):
                q = j * 4 + case
                if off_y:
                    rows.append(first_ref[q, 0:1] if off_x else near_ref[0, q : q + 1])
                else:
                    rows.append(single(below, 8 * q if off_x else 168 + q))
            if off_y:
                rows += [single(above, 8 * q if off_x else 168 + q) for q in range(4 * j, 4 * j + 4)]
            else:
                rows.append(jnp.zeros((4, 256), f32))
            got.append(jnp.concatenate(rows, 0))
        return [next_z(v) for v in got] if off_z else got

    ends = []

    def make_first():
        return element_forces(stiff_ref[0], stiff_ref[1], local.at[8], scale, pick_first)

    def use_first(out):
        flat = [jnp.where(lower, u, v) for u, v in zip(corner_rows(out, 3), corner_rows(out, 1))]
        tall = [jnp.where(lower, u, v) for u, v in zip(corner_rows(out, 7), corner_rows(out, 5))]
        flat, tall = turn_out(scale, flat), turn_out(scale, tall)
        ends.extend(flat[i] + past_z(tall[i]) for i in range(3))

    steps = [(make_first, use_first)]
    for upper in range(2):
        turns = [last_ref[12 + k] if upper else tile(below, 12 + k) for k in range(9)]
        for case in range(4):

            def pick(corner, upper=upper, case=case):
                off_x, off_y, off_z = corner % 2, corner // 2 % 2, corner // 4
                got = []
                for q in (case, 4 + case, 8 + case):
                    if not upper and off_y:
                        v, past = first_ref[q], near_ref[1, q : q + 1]
                    else:
                        source = above if upper else below
                        v, past = tile(source, q), single(source, 192 + q)
                    got.append(jnp.where(row == 7, past, pltpu.roll(v, 7, 0)) if off_x else v)
                return [next_z(v) for v in got] if off_z else got

            def make(upper=upper, case=case, turns=turns, pick=pick):
                slot = local.at[4 * upper + case]
                if upper:
                    return element_forces(across_ref[0], across_ref[1], slot, turns, pick, ORDER[4:])
                return element_forces(stiff_ref[0, 96:192], stiff_ref[1, 96:192], slot, turns, pick)

            def use(out, upper=upper, case=case, turns=turns):
                skipped = 0 if upper else 4
                sides = []
                for off_x in range(2):
                    flat = turn_out(turns, corner_rows(out, off_x + 2 - 2 * upper, skipped))
                    tall = turn_out(turns, corner_rows(out, off_x + 6 - 2 * upper, skipped))
                    sides.append([flat[i] + past_z(tall[i]) for i in range(3)])
                at = 4 * upper + case
                for i in range(3):
                    past = jnp.where(row == 0, ends[i][at : at + 1], pltpu.roll(sides[1][i], 1, 0))
                    (low, high)[upper][i * 4 + case] = sides[0][i] + past

            steps.append((make, use))
    in_turn(steps)

    def residual_of(q, x, force):
        force = force + jnp.where(row == 0, low[q, x : x + 1], 0.0)
        force = force + jnp.where(row == 7, high[q, x : x + 1], 0.0)
        given = loads_ref[q, x]
        left = given - relax_step * (spring * given + force)
        residual_ref[q, x] = left
        return left

    split = inner1_ref.shape[1] - 1
    for q in range(12):
        planes = []
        for x in range(8):
            force = inner1_ref[q, x] if x <= split else inner2_ref[q, x - split]
            if x == split:
                force = force + inner2_ref[q, 0]
            if x in (0, 7):
                force = force + edges_ref[x // 7, q]
            planes.append(residual_of(q, x, force))
        for half in range(2):
            s0 = planes[4 * half] + planes[4 * half + 1]
            s1 = planes[4 * half + 2] + planes[4 * half + 3]
            t0 = s0 + pltpu.roll(s0, 7, 0)
            t1 = s1 + pltpu.roll(s1, 1, 0)
            at = 16 * (q % 6) + 8 * half
            sums[q // 6, at : at + 8] = jnp.where(row % 2 == 0, t0, t1)
    nt = (((1,), (1,)), ((), ()))
    coarse = None
    for half in range(2):
        sums[half, 96:128] = jnp.zeros((32, 256), f32)
        every = sums[half]
        main = every.astype(bf16)
        rest = (every - main.astype(f32)).astype(bf16)
        for part in (main, rest):
            term = lax.dot_general(lift_ref[half], part, nt, preferred_element_type=f32)
            coarse = term if coarse is None else coarse + term
    coarse_ref[...] = coarse.astype(bf16)


def lines_kernel(
    got_ref,
    inverse_ref,
    spread_ref,
    gather_ref,
    keep_ref,
    fold_ref,
    made_ref,
    sent_ref,
    residual_ref,
    rows,
    back,
    stored,
):
    store = pltpu.make_async_copy(made_ref, residual_ref, stored)
    store.start()
    nt = (((1,), (1,)), ((), ()))
    rows[...] = got_ref[...].astype(f32)
    vectors = jnp.zeros((384, 128), f32)
    for half in range(2):
        keep = keep_ref[half].astype(f32)
        keep = jnp.concatenate([keep, keep], 1)
        for pair in range(2 * half, 2 * half + 2):
            part = [rows[pl.ds(2 * pair + k, 32, stride=8), :] for k in range(2)]
            part = jnp.concatenate(part, 1).astype(bf16)
            wide = jnp.dot(spread_ref[...], part, preferred_element_type=f32) * keep
            vectors = vectors + jnp.dot(wide.astype(bf16), fold_ref[pair], preferred_element_type=f32)
    vectors = vectors.astype(bf16)
    line = lax.broadcasted_iota(jnp.int32, (384, 128), 1) // 4
    solved = jnp.zeros((384, 128), f32)
    for k in range(16):
        one = jnp.dot(inverse_ref[k], vectors, preferred_element_type=f32)
        solved = jnp.where(line == k, one, solved)
    solved = solved.astype(bf16)
    for half in range(2):
        keep = keep_ref[half].astype(f32)
        keep = jnp.concatenate([keep, keep], 1)
        for pair in range(2 * half, 2 * half + 2):
            wide = lax.dot_general(solved, fold_ref[pair], nt, preferred_element_type=f32) * keep
            part = jnp.dot(gather_ref[...], wide.astype(bf16), preferred_element_type=f32)
            for k in range(2):
                back[pl.ds(2 * pair + k, 32, stride=8), :] = part[:, 128 * k : 128 * k + 128]
    sent_ref[...] = back[...].astype(bf16)
    store.wait()


def correct_kernel(loads_ref, back_ref, grown_ref, lift_ref, out_ref, made, sent):
    nt = (((1,), (1,)), ((), ()))
    copies = [pltpu.make_async_copy(made.at[q], out_ref.at[q], sent.at[q]) for q in range(12)]
    for half in range(2):
        mine = grown_ref[192 * half : 192 * half + 192]
        mine = lax.dot_general(mine, back_ref[...], nt, preferred_element_type=f32)
        coarse = jnp.dot(mine.astype(bf16), lift_ref[half], preferred_element_type=f32)
        for q in range(6 * half, 6 * half + 6):
            for part in range(4):
                at = 32 * (q % 6) + 8 * part
                added = coarse[at : at + 8]
                for x in (2 * part, 2 * part + 1):
                    made[q, x] = relax_step * loads_ref[q, x] + added
            copies[q].start()
    for copy in copies:
        copy.wait()


def whole(count):
    return [pl.BlockSpec(memory_space=pltpu.VMEM)] * count


def params(mib):
    return pltpu.CompilerParams(vmem_limit_bytes=mib << 20)


def cost(us):
    return pl.CostEstimate(flops=0, bytes_accessed=int(us * 3.0e6), transcendentals=0)


def body(loads, rotations, occupancy, element_matrix, line_inverse):
    table = {name: jnp.asarray(value) for name, value in tables().items()}
    shape = jax.ShapeDtypeStruct
    face = shape((21, 8, 256), bf16)
    plane = lambda count, at: pl.BlockSpec((count, 1, 8, 256), lambda i: (0, at, 0, 0))
    held = [
        pltpu.with_memory_space_constraint(a, pltpu.MemorySpace.HBM)
        for a in (loads, rotations, occupancy, element_matrix)
    ]
    in_hbm = pl.BlockSpec(memory_space=pltpu.MemorySpace.HBM)
    px1, px2, matrix = pl.pallas_call(
        x_faces_kernel,
        in_specs=[in_hbm] * 4,
        out_specs=whole(3),
        out_shape=(face, face, shape((24, 24), f32)),
        scratch_shapes=[
            pltpu.VMEM((2, 12, 8, 256), f32),
            pltpu.VMEM((9, 8, 256), f32),
            pltpu.VMEM((8, 256), jnp.int32),
            pltpu.SemaphoreType.DMA((5,)),
        ],
        compiler_params=params(8),
        name="x_faces",
    )(*held)
    px1 = lax.ppermute(px1, "fine", swaps(FINE, 0))
    px2 = lax.ppermute(px2, "fine", swaps(FINE, 1))
    loads, rotations, occupancy, first, last, stiff, across = pl.pallas_call(
        rows_kernel,
        in_specs=[in_hbm] * 3 + whole(1),
        out_specs=whole(7),
        out_shape=(
            shape(loads.shape, f32),
            shape(rotations.shape, f32),
            shape(occupancy.shape, jnp.int32),
            shape((12, 8, 256), f32),
            shape((21, 8, 256), f32),
            shape((2, 192, 192), bf16),
            shape((2, 96, 96), bf16),
        ),
        scratch_shapes=[pltpu.SemaphoreType.DMA((3,))],
        compiler_params=params(8),
        cost_estimate=cost(2),
        name="rows",
    )(*held[:3], matrix)

    def inner(start, count):
        return pl.pallas_call(
            functools.partial(inner_kernel, start, count),
            in_specs=whole(4),
            out_specs=whole(1)[0],
            out_shape=shape((12, count + 1, 8, 256), f32),
            scratch_shapes=[
                pltpu.VMEM((count + 1, 4, 12, 8, 256), f32),
                pltpu.VMEM((count + 1, 4, 12, 8, 256), f32),
                pltpu.VMEM((4 * count, 2, 192, 256), bf16),
            ],
            compiler_params=params(20),
            cost_estimate=cost(0.8 * count),
            name=f"inner_{start}",
        )(loads, rotations, occupancy, stiff)

    inner1 = inner(0, SPLIT)
    first, inner1 = lax.optimization_barrier((first, inner1))
    face = shape((26, 8, 256), bf16)
    py1, py2, near, far = pl.pallas_call(
        y_faces_kernel,
        in_specs=whole(4),
        out_specs=whole(4),
        out_shape=(face, face, shape((2, 16, 256), f32), shape((16, 256), f32)),
        compiler_params=params(8),
        name="y_faces",
    )(first, last, px1, px2)
    py1 = lax.ppermute(py1, "coarse", swaps(COARSE, 0))
    py2 = lax.ppermute(py2, "coarse", swaps(COARSE, 1))
    inner2 = inner(SPLIT, 7 - SPLIT)
    edges = pl.pallas_call(
        x_edges_kernel,
        grid=(1,),
        in_specs=[
            plane(12, 0),
            plane(12, 7),
            plane(9, 7),
            pl.BlockSpec((1, 8, 256), lambda i: (7, 0, 0)),
            pl.BlockSpec((21, 8, 256), lambda i: (0, 0, 0)),
            pl.BlockSpec((21, 8, 256), lambda i: (0, 0, 0)),
            pl.BlockSpec((2, 192, 192), lambda i: (0, 0, 0)),
        ],
        out_specs=pl.BlockSpec((2, 12, 8, 256), lambda i: (0, 0, 0, 0)),
        out_shape=shape((2, 12, 8, 256), f32),
        scratch_shapes=[
            pltpu.VMEM((4, 4, 12, 8, 256), f32),
            pltpu.VMEM((2, 9, 8, 256), f32),
            pltpu.VMEM((8, 2, 192, 256), bf16),
        ],
        compiler_params=params(12),
        cost_estimate=cost(1.6),
        name="x_edges",
    )(loads, loads, rotations, occupancy, px1, px2, stiff)
    residual, coarse = pl.pallas_call(
        finish_kernel,
        in_specs=whole(13),
        out_specs=whole(2),
        out_shape=(shape((12, 8, 8, 256), f32), shape((256, 128), bf16)),
        scratch_shapes=[
            pltpu.VMEM((208, 256), f32),
            pltpu.VMEM((208, 256), f32),
            pltpu.VMEM((12, 8, 256), f32),
            pltpu.VMEM((12, 8, 256), f32),
            pltpu.VMEM((9, 2, 192, 256), bf16),
            pltpu.VMEM((2, 128, 256), f32),
        ],
        compiler_params=params(16),
        name="finish",
    )(loads, first, last, py1, py2, near, far, stiff, across, table["lift"], inner1, inner2, edges)
    got = lax.all_to_all(coarse.reshape(32, 8, 128), "fine", 0, 0, tiled=True)
    sent, residual = pl.pallas_call(
        lines_kernel,
        in_specs=whole(7),
        out_specs=whole(1) + [pl.BlockSpec(memory_space=pltpu.MemorySpace.HBM)],
        out_shape=(shape((256, 128), bf16), shape((12, 8, 8, 256), f32)),
        scratch_shapes=[
            pltpu.VMEM((256, 128), f32),
            pltpu.VMEM((256, 128), f32),
            pltpu.SemaphoreType.DMA,
        ],
        compiler_params=params(16),
        name="lines",
    )(
        got.reshape(256, 128),
        line_inverse.reshape(16, 384, 384),
        *(table[k] for k in ("spread", "gather", "keep", "fold")),
        residual,
    )
    back = lax.all_to_all(sent.reshape(32, 8, 128), "fine", 0, 0, tiled=True)
    displacement = pl.pallas_call(
        correct_kernel,
        in_specs=whole(4),
        out_specs=pl.BlockSpec(memory_space=pltpu.MemorySpace.HBM),
        out_shape=shape((12, 8, 8, 256), f32),
        scratch_shapes=[pltpu.VMEM((12, 8, 8, 256), f32), pltpu.SemaphoreType.DMA((12,))],
        compiler_params=params(12),
        name="correct",
    )(loads, back.reshape(256, 128), table["grown"], table["lift"])
    return displacement, residual


SPLIT = 3

def solution(mesh):
    in_specs = (
        P(None, "fine", "coarse", None),
        P(None, "fine", "coarse", None),
        P("fine", "coarse", None),
        P(),
        P("coarse", "fine", None, None),
    )
    out_specs = (P(None, "fine", "coarse", None), P(None, "fine", "coarse", None))
    return jax.shard_map(body, mesh=mesh, in_specs=in_specs, out_specs=out_specs, check_vma=False)
```
